32 devices in a mesh: groups: 2 (over y), row: 16 (over z, x, core).
Axes of the slice: x: 2, y: 2, z: 4, core: 2. Of those that a mesh axis runs over, the one named last changes fastest.
Arguments:
- walkers: bfloat16 [64, 1024, 256], P('groups', 'row'), parts along dimension 0, may hold values from -6 to 6
- cholesky: bfloat16 [1024, 1024, 1024], P('groups', 'row'), parts along dimension 0, may hold values from -0.03125 to 0.03125
- slab_index: int32 [4, 64], P('groups'), parts along dimension 0, may hold values from 0 to 511
- fields: bfloat16 [2, 64, 64], P(None, ('groups', 'row')), parts along dimension 1, may hold values from -5 to 5
- counts: int32 [32], P('groups'), parts along dimension 0, may hold values from 1 to 2, as said below
- sources: int32 [4, 32], P('groups'), parts along dimension 0, may hold values from 0 to 31, as said below
Outputs:
- branched: bfloat16 [64, 1024, 256], P('groups', 'row'), parts along dimension 0
The draws below stay inside these ranges and needn't reach their ends.
There are 2 independent parts, one for each index of `groups`. The reference program is written for one: setup_inputs(seed, part) draws one part's arguments, and reference() takes and returns one part's arrays. A program takes and returns all parts, laid end to end along the dimension named above; each array names one. Nothing has to cross between parts.
Inputs may be any that keep to these rules, and one draw needn't show every extreme that they name: counts[d] walkers live in the first counts[d] of the 2 slots d * 2 ... ; some index has all 2 live. For a living slot j, sources[s, j] is a living slot; for any other slot it is j itself.
All inputs are finite; a program needn't handle non-finite values.
Results may differ from the reference program's by a relative error of at most 0.0086.
Values may be sent and summed in bfloat16 or wider, within the bound.
No kernel may reach another device: no remote copies, remote signals or barrier semaphores. Data moves between devices by JAX's collectives and lax.ppermute only.
A program may use at most 192 MiB of HBM per device.

```python
import jax
import jax.numpy as jnp
from jax import lax

NORB = 1024
NEL = 256
SLAB = 64
POOL = 512
WALK_DEV = 2
STEPS = 2
NW = 32
N_ROW = 16


def walker_counts(key):
    levels = jax.random.randint(jax.random.fold_in(key, 11), (N_ROW,), 0, 10)
    counted = 1 + levels * levels * (WALK_DEV - 1) // 81
    fullest = jax.random.randint(jax.random.fold_in(key, 12), (), 0, N_ROW)
    offset = jax.random.randint(jax.random.fold_in(key, 13), (), 1, N_ROW)
    counted = counted.at[fullest].set(WALK_DEV)
    counted = counted.at[(fullest + offset) % N_ROW].set(1)
    return counted.astype(jnp.int32)


def draw_counts(key, part):
    return walker_counts(key)


def draw_sources(key, part):
    counted = walker_counts(key)
    slot_count = WALK_DEV * N_ROW
    slot_ids = jnp.arange(slot_count, dtype=jnp.int32)
    inclusive = jnp.cumsum(counted)
    before = inclusive - counted
    live_total = inclusive[-1]
    ranks = jax.random.randint(jax.random.fold_in(key, 14), (STEPS, slot_count), 0, live_total)
    owners = jnp.sum((inclusive[None, None, :] <= ranks[:, :, None]).astype(jnp.int32), axis=2)
    picked = owners * WALK_DEV + ranks - jnp.take(before, owners)
    living = slot_ids % WALK_DEV < jnp.take(counted, slot_ids // WALK_DEV)
    return jnp.where(living[None, :], picked, slot_ids[None, :]).astype(jnp.int32)


def place_ends(result, key, least, largest):
    dims = result.shape
    place = [jax.random.randint(jax.random.fold_in(key, axis), (), 0, dims[axis]) for axis in range(len(dims))]
    result = result.at[tuple(place)].set(least)
    longest = dims.index(max(dims))
    place[longest] = (place[longest] + 1) % dims[longest]
    return result.at[tuple(place)].set(largest)


def shard_levels(own_key, dims, shards, least, largest):
    level, own = 1.0, jax.random.fold_in(own_key, 6)
    for position, shards_of in shards:
        draws = jnp.exp(jax.random.uniform(jax.random.fold_in(own, position), (shards_of,), jnp.float32, least / len(shards), largest / len(shards)))
        level = level * jnp.repeat(draws, dims[position] // shards_of).reshape([-1 if axis == position else 1 for axis in range(len(dims))])
    return level


def normal_values(own_key, shape, deviation, bound, pieces=(), held_as=jnp.bfloat16):
    loudness = shard_levels(own_key, shape, pieces, -0.22, 0.18) if pieces else 1.0
    array = jax.random.normal(own_key, shape, jnp.float32) * deviation * loudness
    return jnp.minimum(jnp.maximum(array, -bound), bound).astype(held_as)


def setup_inputs(seed: int = 0, part: int = 0) -> dict:
    keys = jax.random.split(jax.random.key(seed), 7)
    part_splits = jax.random.split(jax.random.fold_in(keys[6], part), 7)
    walkers = normal_values(part_splits[0], (NW, NORB, NEL), 1.0, 6.0, ((1, 16),))
    cholesky = normal_values(part_splits[1], (POOL, NORB, NORB), (NORB * SLAB // 2) ** -0.5, 0.03125, ((1, 16),))
    slab_index = place_ends(jax.random.randint(part_splits[2], (STEPS, SLAB), 0, POOL), jax.random.fold_in(part_splits[2], 1), 0, POOL - 1).astype(jnp.int32)
    fields = normal_values(part_splits[3], (STEPS, NW, SLAB), 1.0, 5.0, ((1, 16),))
    counts = draw_counts(jax.random.fold_in(jax.random.fold_in(keys[6], part), 71), part)
    sources = draw_sources(jax.random.fold_in(jax.random.fold_in(keys[6], part), 71), part)
    return {"walkers": walkers, "cholesky": cholesky, "slab_index": slab_index, "fields": fields, "counts": counts, "sources": sources}


def taylor_step(potential, initial):
    summed = initial.astype(jnp.float32)
    term_now = initial
    for degree in range(1, 5):
        product = jnp.dot(potential, term_now, preferred_element_type=jnp.float32) / degree
        summed = summed + product
        term_now = product.astype(jnp.bfloat16)
    return summed.astype(jnp.bfloat16)


def reference(walkers, cholesky, slab_index, fields, counts, sources):
    slot_count = walkers.shape[0]
    per_device = slot_count // N_ROW
    block_size = per_device * 8
    slot_ids = jnp.arange(slot_count, dtype=jnp.int32)
    living = (slot_ids % per_device) < jnp.take(counts, slot_ids // per_device)
    current = walkers
    for step_number in range(STEPS):
        chosen = jnp.take(cholesky, slab_index[step_number], axis=0).reshape(SLAB, NORB * NORB)

        def one_block(packed):
            block_fields, block_walkers, block_living = packed
            joined = jnp.dot(block_fields, chosen, preferred_element_type=jnp.float32)
            potentials = lax.optimization_barrier(joined.astype(jnp.bfloat16)).reshape(block_size, NORB, NORB)

            def one_walker(inner):
                matrix, initial, is_live = inner
                return lax.cond(is_live, lambda pair: taylor_step(pair[0], pair[1]), lambda pair: jnp.zeros_like(pair[1]), (matrix, initial))

            return lax.map(one_walker, (potentials, block_walkers, block_living))

        propagated = lax.map(one_block, (fields[step_number].reshape(-1, block_size, SLAB), current.reshape(-1, block_size, NORB, NEL), living.reshape(-1, block_size)))
        current = jnp.take(propagated.reshape(slot_count, NORB, NEL), sources[step_number], axis=0)
    return current
```

```python
import functools

import jax
import jax.numpy as jnp
from jax import lax
from jax.experimental import pallas as pl
from jax.experimental.pallas import tpu as pltpu
from jax.sharding import PartitionSpec as P

ORDER = 4
ROWS = 16
SMEM = pl.BlockSpec(memory_space=pltpu.SMEM)
VMEM = pl.BlockSpec(memory_space=pltpu.VMEM)
ANY = pl.BlockSpec(memory_space=pl.ANY)


def plan_kernel(per_device, counts, sources, first, second, place, total, order):
    slots = place.shape[0]

    def clear(slot, carry):
        order[slot] = -1
        first[slot] = 0
        second[slot] = 0
        return carry

    lax.fori_loop(0, slots, clear, 0)

    def alive(slot):
        return slot % per_device < counts[slot // per_device]

    def mark(slot, carry):
        @pl.when(alive(slot))
        def _():
            order[sources[1, slot]] = 0

        return carry

    lax.fori_loop(0, slots, mark, 0)

    def number(slot, found):
        kept = order[slot] >= 0

        @pl.when(kept)
        def _():
            order[slot] = found
            first[found] = sources[0, slot]
            second[found] = slot

        return found + kept.astype(jnp.int32)

    total[0] = lax.fori_loop(0, slots, number, jnp.int32(0))

    def look(slot, carry):
        place[slot] = jnp.where(alive(slot), order[sources[1, slot]], -1)
        return carry

    lax.fori_loop(0, slots, look, 0)


def plan(counts, sources, per_device):
    slots = sources.shape[1]
    vector = jax.ShapeDtypeStruct((slots,), jnp.int32)
    return pl.pallas_call(
        functools.partial(plan_kernel, per_device),
        out_shape=(vector, vector, vector, jax.ShapeDtypeStruct((1,), jnp.int32)),
        in_specs=[SMEM, SMEM],
        out_specs=(SMEM, SMEM, SMEM, SMEM),
        scratch_shapes=[pltpu.SMEM((slots,), jnp.int32)],
    )(counts, sources)


def pick_kernel(first, base, walkers, picked, semaphore):
    for chain in range(picked.shape[0]):
        pltpu.make_async_copy(
            walkers.at[first[base[0] + chain]], picked.at[chain], semaphore
        ).start()
    pltpu.make_async_copy(picked, picked, semaphore).wait()


def pick(walkers, first, base, chains):
    shape = (chains,) + walkers.shape[1:]
    return pl.pallas_call(
        pick_kernel,
        out_shape=jax.ShapeDtypeStruct(shape, walkers.dtype),
        in_specs=[SMEM, SMEM, ANY],
        out_specs=VMEM,
        scratch_shapes=[pltpu.SemaphoreType.DMA],
    )(first, base, walkers)


def potential_kernel(
    chains, step, chosen, base, slab, fields, cholesky, out, blocks, left, semaphores
):
    vectors = blocks.shape[1]
    block = pl.program_id(0)

    def fetch(block, slot):
        def one(vector, carry):
            pltpu.make_async_copy(
                cholesky.at[slab[step, vector], pl.ds(block * ROWS, ROWS), :],
                blocks.at[slot, vector],
                semaphores.at[slot],
            ).start()
            return carry

        lax.fori_loop(0, vectors, one, 0, unroll=8)

    @pl.when(block == 0)
    def _():
        fetch(0, 0)
        slots = fields.shape[0]
        row = lax.broadcasted_iota(jnp.int32, (chains * ROWS, slots), 0) // ROWS
        wanted = jnp.zeros((chains * ROWS, slots), jnp.int32)
        for chain in range(chains):
            wanted = jnp.where(row == chain, chosen[base[0] + chain], wanted)
        column = lax.broadcasted_iota(jnp.int32, (chains * ROWS, slots), 1)
        rows_of = (wanted == column).astype(jnp.float32).astype(jnp.bfloat16)
        repeated = jnp.dot(
            rows_of, fields[...], preferred_element_type=jnp.float32
        ).astype(jnp.bfloat16)
        spread = (
            lax.broadcasted_iota(jnp.int32, (vectors, vectors * ROWS), 0)
            == lax.broadcasted_iota(jnp.int32, (vectors, vectors * ROWS), 1) // ROWS
        )
        wide = jnp.dot(
            repeated,
            spread.astype(jnp.float32).astype(jnp.bfloat16),
            preferred_element_type=jnp.float32,
        )
        same = (
            lax.broadcasted_iota(jnp.int32, wide.shape, 0) % ROWS
            == lax.broadcasted_iota(jnp.int32, wide.shape, 1) % ROWS
        )
        left[...] = jnp.where(same, wide, 0.0).astype(jnp.bfloat16)

    @pl.when(block + 1 < pl.num_programs(0))
    def _():
        fetch(block + 1, (block + 1) % 2)

    slot = block % 2
    pltpu.make_async_copy(blocks.at[slot], blocks.at[slot], semaphores.at[slot]).wait()
    orbitals = out.shape[2]
    right = blocks[slot].reshape(vectors * ROWS, orbitals)
    product = jnp.dot(left[...], right, preferred_element_type=jnp.float32)
    out[...] = product.astype(jnp.bfloat16).reshape(chains, ROWS, orbitals)


def potential_rows(cholesky, slab, fields, chosen, base, step, chains):
    local_rows, orbitals = cholesky.shape[1:]
    vectors = slab.shape[1]
    if local_rows % ROWS:
        members = lax.dynamic_slice_in_dim(chosen, base[0], chains)
        return (
            jnp.dot(
                jnp.take(fields, members, axis=0, mode="clip"),
                jnp.take(cholesky, slab[step], axis=0, mode="clip").reshape(vectors, -1),
                preferred_element_type=jnp.float32,
            )
            .astype(jnp.bfloat16)
            .reshape(chains, local_rows, orbitals)
        )
    return pl.pallas_call(
        functools.partial(potential_kernel, chains, step),
        out_shape=jax.ShapeDtypeStruct((chains, local_rows, orbitals), jnp.bfloat16),
        grid=(local_rows // ROWS,),
        in_specs=[SMEM, SMEM, SMEM, VMEM, ANY],
        out_specs=pl.BlockSpec((chains, ROWS, orbitals), lambda block: (0, block, 0)),
        scratch_shapes=[
            pltpu.VMEM((2, vectors, ROWS, orbitals), jnp.bfloat16),
            pltpu.VMEM((chains * ROWS, vectors * ROWS), jnp.bfloat16),
            pltpu.SemaphoreType.DMA((2,)),
        ],
        cost_estimate=pl.CostEstimate(
            flops=2 * chains * ROWS * vectors * local_rows * orbitals,
            bytes_accessed=2 * (vectors + chains) * local_rows * orbitals,
            transcendentals=0,
        ),
        compiler_params=pltpu.CompilerParams(vmem_limit_bytes=32 << 20),
    )(chosen, base, slab, fields, cholesky)


def taylor_kernel(matrix, initial, out, summed, term):
    tile = min(256, matrix.shape[0])
    for degree in range(1, ORDER + 1):
        source = initial if degree == 1 else term.at[degree % 2]
        for start in range(0, matrix.shape[0], tile):
            rows = slice(start, start + tile)
            product = jnp.dot(
                matrix[rows, :], source[...], preferred_element_type=jnp.float32
            ) * (1.0 / degree)
            before = initial[rows, :].astype(jnp.float32) if degree == 1 else summed[rows, :]
            if degree == ORDER:
                out[rows, :] = (before + product).astype(jnp.bfloat16)
            else:
                summed[rows, :] = before + product
                term[(degree + 1) % 2, rows, :] = product.astype(jnp.bfloat16)


def taylor(matrix, initial):
    rows, columns = initial.shape
    return pl.pallas_call(
        taylor_kernel,
        out_shape=jax.ShapeDtypeStruct(initial.shape, jnp.bfloat16),
        in_specs=[VMEM, VMEM],
        out_specs=VMEM,
        scratch_shapes=[
            pltpu.VMEM((rows, columns), jnp.float32),
            pltpu.VMEM((2, rows, columns), jnp.bfloat16),
        ],
        cost_estimate=pl.CostEstimate(
            flops=2 * ORDER * rows * rows * columns,
            bytes_accessed=2 * rows * (rows + 2 * columns),
            transcendentals=0,
        ),
        compiler_params=pltpu.CompilerParams(vmem_limit_bytes=32 << 20),
    )(matrix, initial)


def exchange(array):
    return lax.all_to_all(array, "row", split_axis=0, concat_axis=0, tiled=True)


def on_device(walkers, cholesky, slab_index, fields, counts, sources):
    local_rows, columns = walkers.shape[1:]
    orbitals = cholesky.shape[2]
    steps, per_device, vectors = fields.shape
    devices = lax.axis_size("row")
    slots = per_device * devices
    first, second, place, total = plan(counts, sources, per_device)
    sent = jnp.broadcast_to(
        fields.reshape(1, steps * per_device, vectors), (devices, steps * per_device, vectors)
    )
    all_fields = (
        exchange(sent)
        .reshape(devices, steps, per_device, vectors)
        .swapaxes(0, 1)
        .reshape(steps, slots, vectors)
    )

    def one_pass(base):
        initial = exchange(pick(walkers, first, base, devices))
        early = exchange(
            potential_rows(cholesky, slab_index, all_fields[0], first, base, 0, devices)
        )
        late = exchange(
            potential_rows(cholesky, slab_index, all_fields[1], second, base, 1, devices)
        )
        current = initial.reshape(orbitals, columns)
        for matrix in (early, late):
            current = taylor(matrix.reshape(orbitals, orbitals), current)
        return exchange(current.reshape(devices, local_rows, columns))

    def select(returned, base):
        own = place - base[0]
        hit = jnp.logical_and(own >= 0, own < devices)
        return hit[:, None, None], jnp.take(returned, own, axis=0, mode="clip")

    base = jnp.zeros((1,), jnp.int32)
    hit, rows = select(one_pass(base), base)
    branched = jnp.where(hit, rows, jnp.zeros_like(rows))

    def another(number, branched):
        base = jnp.full((1,), number * devices, jnp.int32)
        hit, rows = select(one_pass(base), base)
        return jnp.where(hit, rows, branched)

    return lax.fori_loop(1, (total[0] + devices - 1) // devices, another, branched)


def solution(mesh):
    in_specs = (
        P("groups", "row", None),
        P("groups", "row", None),
        P("groups", None),
        P(None, ("groups", "row"), None),
        P("groups"),
        P("groups", None),
    )
    out_specs = P("groups", "row", None)
    return jax.shard_map(
        on_device, mesh=mesh, in_specs=in_specs, out_specs=out_specs, check_vma=False
    )
```

```python
import functools

import jax
import jax.numpy as jnp
from jax import lax
from jax.experimental import pallas as pl
from jax.experimental.pallas import tpu as pltpu
from jax.sharding import PartitionSpec as P


ORDER = 4
ROWS = 16
SMEM = pl.BlockSpec(memory_space=pltpu.SMEM)
VMEM = pl.BlockSpec(memory_space=pltpu.VMEM)
ANY = pl.BlockSpec(memory_space=pl.ANY)


def params(mebibytes=40):
    return pltpu.CompilerParams(vmem_limit_bytes=mebibytes << 20)


def plan_kernel(per_device, counts, sources, lists, place, total, order):
    slots = place.shape[0]

    def clear(slot, carry):
        order[slot] = -1
        lists[0, slot] = 0
        lists[1, slot] = 0
        return carry

    lax.fori_loop(0, slots, clear, 0)

    def alive(slot):
        return slot % per_device < counts[slot // per_device]

    def mark(slot, carry):
        @pl.when(alive(slot))
        def _():
            order[sources[1, slot]] = 0

        return carry

    lax.fori_loop(0, slots, mark, 0)

    def number(slot, found):
        kept = order[slot] >= 0

        @pl.when(kept)
        def _():
            order[slot] = found
            lists[0, found] = sources[0, slot]
            lists[1, found] = slot

        return found + kept.astype(jnp.int32)

    total[0] = lax.fori_loop(0, slots, number, jnp.int32(0))

    def look(slot, carry):
        place[slot] = jnp.where(alive(slot), order[sources[1, slot]], -1)
        return carry

    lax.fori_loop(0, slots, look, 0)


def plan(counts, sources, per_device):
    slots = sources.shape[1]
    vector = jax.ShapeDtypeStruct((slots,), jnp.int32)
    return pl.pallas_call(
        functools.partial(plan_kernel, per_device),
        out_shape=(
            jax.ShapeDtypeStruct((2, slots), jnp.int32),
            vector,
            jax.ShapeDtypeStruct((1,), jnp.int32),
        ),
        in_specs=[SMEM, SMEM],
        out_specs=(SMEM, SMEM, SMEM),
        scratch_shapes=[pltpu.SMEM((slots,), jnp.int32)],
    )(counts, sources)


def target_of(small, step, chips, device):
    chip, core = device // 2, device % 2
    if small and core:
        return chip % 2, chips + chip // 2
    return step, chip + core * chips


def potential_kernel(targets, spread, per_device, pieces, walked, me, lists, base, slab, *refs):
    fields, refs = refs[:pieces], refs[pieces:]
    cholesky, refs = refs[0], refs[1:]
    walkers, refs = (refs[0], refs[1:]) if walked else (None, refs)
    scratch = refs[-4 - walked :]
    blocks, left, held, semaphores = scratch[:4]
    picked = scratch[4] if walked else None
    outs = refs[: -4 - walked]
    steps = sorted({step for step, _ in targets})
    vectors = blocks.shape[1]
    halves = semaphores.shape[0] - 1
    half_rows = blocks.shape[2] // halves
    orbitals = blocks.shape[3]
    devices = held.shape[0]
    block = pl.program_id(0)

    def slot_of(number):
        step, chain = targets[number]
        if spread:
            chain = (me[0] // 2) ^ chain
        return lists[step, base[0] + chain]

    @pl.when(block == 0)
    def _():
        for half in range(halves):
            rows = pl.ds(half * half_rows, half_rows)
            for which, step in enumerate(steps):

                def one(vector, carry, rows=rows, half=half, which=which, step=step):
                    pltpu.make_async_copy(
                        cholesky.at[slab[step, vector], rows, :],
                        blocks.at[which, vector, rows, :],
                        semaphores.at[half],
                    ).start()
                    return carry

                lax.fori_loop(0, vectors, one, 0, unroll=8)
        if walked:
            for number in range(len(targets)):
                pltpu.make_async_copy(
                    walkers.at[slot_of(number)], picked.at[number], semaphores.at[halves]
                ).start()
        part = devices // pieces
        for piece in range(pieces):
            held[piece * part : (piece + 1) * part, :] = fields[piece][...].astype(jnp.float32)
        widen = (
            lax.broadcasted_iota(jnp.int32, (vectors, vectors * ROWS), 0)
            == lax.broadcasted_iota(jnp.int32, (vectors, vectors * ROWS), 1) // ROWS
        )
        widen = widen.astype(jnp.float32).astype(jnp.bfloat16)
        start = 0
        for step in steps:
            members = [number for number, target in enumerate(targets) if target[0] == step]
            shape = (len(members) * ROWS, devices)
            row = lax.broadcasted_iota(jnp.int32, shape, 0) // ROWS
            column = lax.broadcasted_iota(jnp.int32, shape, 1)
            wanted = jnp.zeros(shape, jnp.int32)
            for place, number in enumerate(members):
                slot = slot_of(number)
                there = ((slot // per_device) ^ me[0]) * per_device + slot % per_device
                wanted = jnp.where(row == place, there, wanted)
            repeated = jnp.zeros((shape[0], vectors), jnp.float32)
            for within in range(per_device):
                rows_of = (wanted == column * per_device + within).astype(jnp.float32)
                first = (step * per_device + within) * vectors
                repeated = repeated + jnp.dot(
                    rows_of.astype(jnp.bfloat16),
                    held[:, first : first + vectors].astype(jnp.bfloat16),
                    preferred_element_type=jnp.float32,
                )
            wide = jnp.dot(
                repeated.astype(jnp.bfloat16), widen, preferred_element_type=jnp.float32
            )
            same = (
                lax.broadcasted_iota(jnp.int32, wide.shape, 0) % ROWS
                == lax.broadcasted_iota(jnp.int32, wide.shape, 1) % ROWS
            )
            left[start : start + shape[0], :] = jnp.where(same, wide, 0.0).astype(jnp.bfloat16)
            start += shape[0]
        if walked:
            pltpu.make_async_copy(picked, picked, semaphores.at[halves]).wait()

    for half in range(halves):

        @pl.when(block == half * (half_rows // ROWS))
        def _():
            view = blocks.at[:, :, pl.ds(half * half_rows, half_rows), :]
            pltpu.make_async_copy(view, view, semaphores.at[half]).wait()

    rows = pl.ds(block * ROWS, ROWS)
    start = 0
    for which, step in enumerate(steps):
        members = [number for number, target in enumerate(targets) if target[0] == step]
        right = blocks[which, :, rows, :].reshape(vectors * ROWS, orbitals)
        end = start + len(members) * ROWS
        product = jnp.dot(
            left[start:end, :], right, preferred_element_type=jnp.float32
        ).astype(jnp.bfloat16)
        start = end
        for place, number in enumerate(members):
            out = outs[number] if spread else outs[0].at[number]
            out[:, :orbitals] = product[place * ROWS : (place + 1) * ROWS]
            if walked:
                out[:, orbitals:] = picked[number, rows, :]


def potential_rows(
    cholesky, slab, fields, walkers, lists, me, base, targets, spread, per_device, devices
):
    local_rows, orbitals = cholesky.shape[1:]
    vectors = slab.shape[1]
    count = len({step for step, _ in targets})
    walked = walkers is not None
    width = orbitals + (walkers.shape[2] if walked else 0)
    halves = 2 if local_rows % (2 * ROWS) == 0 else 1
    scratch = [
        pltpu.VMEM((count, vectors, local_rows, orbitals), jnp.bfloat16),
        pltpu.VMEM((len(targets) * ROWS, vectors * ROWS), jnp.bfloat16),
        pltpu.VMEM((devices, fields[0].shape[1]), jnp.float32),
        pltpu.SemaphoreType.DMA((halves + 1,)),
    ]
    if walked:
        scratch.append(pltpu.VMEM((len(targets),) + walkers.shape[1:], jnp.bfloat16))
    if spread:
        shapes = [jax.ShapeDtypeStruct((local_rows, width), jnp.bfloat16)] * len(targets)
        specs = [pl.BlockSpec((ROWS, width), lambda block: (block, 0))] * len(targets)
    else:
        shapes = jax.ShapeDtypeStruct((len(targets), local_rows, width), jnp.bfloat16)
        specs = pl.BlockSpec((len(targets), ROWS, width), lambda block: (0, block, 0))
    return pl.pallas_call(
        functools.partial(
            potential_kernel, targets, spread, per_device, len(fields), walked
        ),
        out_shape=shapes,
        grid=(local_rows // ROWS,),
        in_specs=[SMEM] * 4 + [VMEM] * len(fields) + [ANY] * (1 + walked),
        out_specs=specs,
        scratch_shapes=scratch,
        cost_estimate=pl.CostEstimate(
            flops=2 * len(targets) * ROWS * vectors * local_rows * orbitals,
            bytes_accessed=2 * (count * vectors + len(targets)) * local_rows * orbitals,
            transcendentals=0,
        ),
        compiler_params=params(),
    )(me, lists, base, slab, *fields, cholesky, *((walkers,) if walked else ()))


def taylor_kernel(mode, chips, me, joint, *refs):
    parts, refs = (refs[:chips], refs[chips:]) if mode == "small" else ((), refs)
    across, refs = (refs[: chips], refs[chips:]) if mode == "small" else ((), refs)
    starts, refs = refs[: {"first": 0, "large": 1, "small": 2}[mode]], refs[
        {"first": 0, "large": 1, "small": 2}[mode] :
    ]
    out, matrix, begun, summed, term, semaphores, ready = refs
    devices, local = joint.shape[:2]
    rows, columns = summed.shape
    tiles = devices // 4
    tile = rows // tiles

    def view(number):
        return matrix.at[pl.ds(pl.multiple_of(number * tile, tile), tile), :]

    def copy_joint(number):
        for device in range(4):
            pltpu.make_async_copy(
                joint.at[4 * number + device, :, pl.ds(0, rows)],
                matrix.at[pl.ds(pl.multiple_of((4 * number + device) * local, local), local), :],
                semaphores.at[number],
            ).start()

    def copy_begun(source):
        pltpu.make_async_copy(source, begun, ready).start()

    if mode == "first":
        for device in range(devices):
            pltpu.make_async_copy(
                joint.at[device, :, pl.ds(rows, columns)],
                begun.at[pl.ds(device * local, local), :],
                ready,
            ).start()
    if mode == "large":
        copy_begun(starts[0])
    if mode == "small":
        own = me[0] % 2 == 0

        @pl.when(own)
        def _():
            copy_begun(starts[0])
            for chip in range(chips):
                for core in range(2):
                    device = me[0] ^ (2 * chip + core)
                    pltpu.make_async_copy(
                        across[chip] if core else parts[chip],
                        matrix.at[pl.ds(pl.multiple_of(device * local, local), local), :],
                        semaphores.at[device // 4],
                    ).start()

        @pl.when(jnp.logical_not(own))
        def _():
            copy_begun(starts[1])
            for number in range(tiles):
                copy_joint(number)
    else:
        for number in range(tiles):
            copy_joint(number)
    pltpu.make_async_copy(begun, begun, ready).wait()
    for degree in range(1, ORDER + 1):
        for number in range(tiles):
            span = slice(number * tile, (number + 1) * tile)
            if degree == 1:
                pltpu.make_async_copy(view(number), view(number), semaphores.at[number]).wait()
                source = begun[...]
                before = begun[span, :].astype(jnp.float32)
            else:
                source = term[degree % 2]
                before = summed[span, :]
            product = jnp.dot(
                matrix[span, :], source, preferred_element_type=jnp.float32
            ) * (1.0 / degree)
            if degree < ORDER:
                summed[span, :] = before + product
                term[(degree + 1) % 2, span, :] = product.astype(jnp.bfloat16)
            else:
                out[span, :] = (before + product).astype(jnp.bfloat16)


def taylor(mode, me, joint, parts, across, starts, columns):
    devices, local = joint.shape[:2]
    rows = devices * local
    chips = devices // 2
    return pl.pallas_call(
        functools.partial(taylor_kernel, mode, chips),
        out_shape=jax.ShapeDtypeStruct((rows, columns), jnp.bfloat16),
        in_specs=[SMEM] + [ANY] * (1 + len(parts) + len(across) + len(starts)),
        out_specs=VMEM,
        scratch_shapes=[
            pltpu.VMEM((rows, rows), jnp.bfloat16),
            pltpu.VMEM((rows, columns), jnp.bfloat16),
            pltpu.VMEM((rows, columns), jnp.float32),
            pltpu.VMEM((2, rows, columns), jnp.bfloat16),
            pltpu.SemaphoreType.DMA((devices // 4,)),
            pltpu.SemaphoreType.DMA,
        ],
        cost_estimate=pl.CostEstimate(
            flops=2 * ORDER * rows * rows * columns,
            bytes_accessed=2 * rows * (rows + 3 * columns),
            transcendentals=0,
        ),
        compiler_params=params(),
    )(me, joint, *parts, *across, *starts)


def select_kernel(small, kept, place, base, returned, *refs):
    out = refs[-1]
    chips = returned.shape[0] // 2
    capacity = chips * 3 // 2 if small else chips * 2

    def one(slot, carry):
        chain = place[slot] - base[0]
        hit = jnp.logical_and(chain >= 0, chain < capacity)
        chain = jnp.clip(chain, 0, capacity - 1)
        other = 2 * (chain - chips)
        owner = jnp.where(chain < chips, 2 * chain, 2 * other + 3 if small else other + 1)

        @pl.when(hit)
        def _():
            out[slot] = returned[owner]

        @pl.when(jnp.logical_not(hit))
        def _():
            out[slot] = refs[0][slot] if kept else jnp.zeros(out.shape[1:], out.dtype)

        return carry

    lax.fori_loop(0, out.shape[0], one, 0)


def select(place, base, returned, before, small):
    kept = before is not None
    slots = place.shape[0]
    return pl.pallas_call(
        functools.partial(select_kernel, small, kept),
        out_shape=jax.ShapeDtypeStruct((slots,) + returned.shape[1:], returned.dtype),
        in_specs=[SMEM] * 2 + [VMEM] * (1 + kept),
        out_specs=VMEM,
        compiler_params=params(),
    )(place, base, returned, *((before,) if kept else ()))


def swap(array, distance, devices, senders=lambda device: True):
    pairs = [(d, d ^ distance) for d in range(devices) if senders(d)]
    return lax.ppermute(array, "row", pairs)


def share_fields(fields, devices):
    rows, distance = fields.reshape(1, -1), 1
    while distance * 4 < devices:
        rows = jnp.concatenate([rows, swap(rows, distance, devices)])
        distance *= 2
    return [rows] + [swap(rows, far, devices) for far in range(distance, devices, distance)]


def by_chips(walkers, cholesky, slab_index, fields, counts, sources):
    local_rows, columns = walkers.shape[1:]
    per_device = fields.shape[1]
    devices = lax.axis_size("row")
    chips = devices // 2
    me = lax.axis_index("row").reshape(1).astype(jnp.int32)
    lists, place, total = plan(counts, sources, per_device)
    pieces = share_fields(fields, devices)

    def one_pass(small, base, before):
        def rows_of(targets, spread, moved):
            return potential_rows(
                cholesky, slab_index, pieces, moved, lists, me, base, targets, spread,
                per_device, devices,
            )

        def all_targets(step):
            return tuple(target_of(small, step, chips, d) for d in range(devices))

        rows = rows_of(all_targets(0), False, walkers)
        joint = exchange(rows)
        if small:
            late = rows_of(tuple((1, m) for m in range(chips)), True, None)
            parts = [late[0]] + [
                swap(late[m], 2 * m, devices, lambda d: d % 2 == 0)
                for m in range(1, chips)
            ]
            across = [swap(late[m], 2 * m + 1, devices, lambda d: d % 2 == 1) for m in range(chips)]
            current = taylor("first", me, joint, [], [], [], columns)
            moved = swap(current, 2, devices, lambda d: d % 4 == 1)
            advanced = taylor("small", me, joint, parts, across, [current, moved], columns)
        else:
            rows = rows_of(all_targets(1), False, None)
            late = exchange(rows)
            current = taylor("first", me, joint, [], [], [], columns)
            advanced = taylor("large", me, late, [], [], [current], columns)
        returned = exchange(advanced.reshape(devices, local_rows, columns))
        return select(place, base, returned, before, small)

    def small():
        return one_pass(True, jnp.zeros((1,), jnp.int32), None)

    def large():
        def another(turn, before):
            return one_pass(False, jnp.full((1,), turn * devices, jnp.int32), before)

        turns = (total[0] + devices - 1) // devices
        return lax.fori_loop(0, turns, another, jnp.zeros_like(walkers))

    return lax.cond(total[0] <= chips * 3 // 2, small, large)


def exchange(array):
    return lax.all_to_all(array, "row", split_axis=0, concat_axis=0, tiled=True)


def taylor_step(potential, initial):
    summed = initial.astype(jnp.float32)
    term_now = initial
    for degree in range(1, ORDER + 1):
        product = jnp.dot(potential, term_now, preferred_element_type=jnp.float32) / degree
        summed = summed + product
        term_now = product.astype(jnp.bfloat16)
    return summed.astype(jnp.bfloat16)


def by_all_to_alls(walkers, cholesky, slab_index, fields, counts, sources):
    local_rows, columns = walkers.shape[1:]
    orbitals = cholesky.shape[2]
    per_device = fields.shape[1]
    devices = lax.axis_size("row")
    (first, second), place, total = plan(counts, sources, per_device)
    all_fields = lax.all_gather(fields, "row", axis=1, tiled=True)

    def rows_of(chosen, step, base):
        members = lax.dynamic_slice_in_dim(chosen, base, devices)
        vectors = jnp.take(cholesky, slab_index[step], axis=0, mode="clip")
        rows = jnp.dot(
            jnp.take(all_fields[step], members, axis=0, mode="clip"),
            vectors.reshape(vectors.shape[0], -1),
            preferred_element_type=jnp.float32,
        )
        return rows.astype(jnp.bfloat16).reshape(devices, local_rows, orbitals)

    def another(turn, before):
        base = turn * devices
        members = lax.dynamic_slice_in_dim(first, base, devices)
        current = exchange(jnp.take(walkers, members, axis=0, mode="clip"))
        current = current.reshape(orbitals, columns)
        for step, chosen in enumerate((first, second)):
            matrix = exchange(rows_of(chosen, step, base))
            current = taylor_step(matrix.reshape(orbitals, orbitals), current)
        returned = exchange(current.reshape(devices, local_rows, columns))
        own = place - base
        hit = jnp.logical_and(own >= 0, own < devices)
        rows = jnp.take(returned, own, axis=0, mode="clip")
        return jnp.where(hit[:, None, None], rows, before)

    turns = (total[0] + devices - 1) // devices
    return lax.fori_loop(0, turns, another, jnp.zeros_like(walkers))


def on_device(walkers, cholesky, slab_index, fields, counts, sources):
    devices = lax.axis_size("row")
    power = devices & (devices - 1) == 0
    if power and 8 <= devices <= 32 and cholesky.shape[1] % ROWS == 0 and walkers.shape[2] % 128 == 0:
        route = by_chips
    else:
        route = by_all_to_alls
    return route(walkers, cholesky, slab_index, fields, counts, sources)


def solution(mesh):
    in_specs = (
        P("groups", "row", None),
        P("groups", "row", None),
        P("groups", None),
        P(None, ("groups", "row"), None),
        P("groups"),
        P("groups", None),
    )
    out_specs = P("groups", "row", None)
    return jax.shard_map(
        on_device, mesh=mesh, in_specs=in_specs, out_specs=out_specs, check_vma=False
    )
```

```python
import functools

import jax
import jax.numpy as jnp
from jax import lax
from jax.experimental import pallas as pl
from jax.experimental.pallas import tpu as pltpu
from jax.sharding import PartitionSpec as P


ORDER = 4
ROWS = 16
SMEM = pl.BlockSpec(memory_space=pltpu.SMEM)
VMEM = pl.BlockSpec(memory_space=pltpu.VMEM)
ANY = pl.BlockSpec(memory_space=pl.ANY)


def params(mebibytes=40):
    return pltpu.CompilerParams(vmem_limit_bytes=mebibytes << 20)


def plan_kernel(
    per_device, counts, sources, lists, place, jobs, owned, total, order, lead, twin, owner
):
    slots, devices = place.shape[0], counts.shape[0]
    chips = devices // 2

    def clear(slot, carry):
        order[slot] = -1
        lead[slot] = -1
        lists[0, slot] = 0
        lists[1, slot] = 0
        return carry

    lax.fori_loop(0, slots, clear, 0)

    def alive(slot):
        return slot % per_device < counts[slot // per_device]

    def mark(slot, carry):
        @pl.when(alive(slot))
        def _():
            order[sources[1, slot]] = 0

        return carry

    lax.fori_loop(0, slots, mark, 0)

    def number(slot, found):
        count, twins = found
        kept = order[slot] >= 0
        start = sources[0, slot]
        other = lead[start]
        paired = jnp.logical_and(kept, other >= 0)

        @pl.when(kept)
        def _():
            order[slot] = count
            lists[0, count] = start
            lists[1, count] = slot

        @pl.when(paired)
        def _():
            twin[other] = count
            twin[count] = -2
            lead[start] = -1

        @pl.when(jnp.logical_and(kept, other < 0))
        def _():
            twin[count] = -1
            lead[start] = count

        return count + kept.astype(jnp.int32), twins + paired.astype(jnp.int32)

    count, twins = lax.fori_loop(0, slots, number, (jnp.int32(0), jnp.int32(0)))
    total[0] = count
    leads, pair = count - twins, (twins + 1) // 2
    fits = leads - chips <= jnp.maximum(chips // 2 - pair, 0)
    total[1] = fits.astype(jnp.int32)

    def empty(device, carry):
        for row in range(4):
            jobs[row, device] = 0
        return carry

    lax.fori_loop(0, devices, empty, 0)

    @pl.when(fits)
    def _():
        def assign(chain, taken):
            with_twin, without, more = taken
            other = twin[chain]
            leading = other > -2
            doubled = other >= 0
            single = other == -1
            chip = jnp.where(doubled, with_twin, without)
            inside = jnp.logical_and(leading, chip < chips)
            outside = jnp.logical_and(single, chip >= chips)

            @pl.when(inside)
            def _():
                jobs[1, 2 * chip] = lists[0, chain]
                jobs[2, chip] = lists[1, chain]
                owner[chain] = 2 * chip

            @pl.when(doubled)
            def _():
                jobs[0, 2 * chip + 1] = 1
                jobs[1, 2 * chip + 1] = lists[1, other]
                jobs[3, chip] = 1
                owner[other] = 2 * chip + 1

            @pl.when(outside)
            def _():
                jobs[1, 4 * more + 1] = lists[0, chain]
                jobs[0, 4 * more + 3] = 1
                jobs[1, 4 * more + 3] = lists[1, chain]
                owner[chain] = 4 * more + 3

            return (
                with_twin + doubled.astype(jnp.int32),
                without + jnp.logical_and(single, inside).astype(jnp.int32),
                more + outside.astype(jnp.int32),
            )

        lax.fori_loop(0, count, assign, (jnp.int32(0), twins, pair))

    def look(slot, carry):
        chain = jnp.where(alive(slot), order[sources[1, slot]], -1)
        place[slot] = chain
        owned[slot] = jnp.where(
            jnp.logical_and(chain >= 0, fits), owner[jnp.maximum(chain, 0)], -1
        )
        return carry

    lax.fori_loop(0, slots, look, 0)


def plan(counts, sources, per_device):
    slots, devices = sources.shape[1], counts.shape[0]
    vector = jax.ShapeDtypeStruct((slots,), jnp.int32)
    return pl.pallas_call(
        functools.partial(plan_kernel, per_device),
        out_shape=(
            jax.ShapeDtypeStruct((2, slots), jnp.int32),
            vector,
            jax.ShapeDtypeStruct((4, devices), jnp.int32),
            vector,
            jax.ShapeDtypeStruct((2,), jnp.int32),
        ),
        in_specs=[SMEM, SMEM],
        out_specs=(SMEM,) * 5,
        scratch_shapes=[pltpu.SMEM((slots,), jnp.int32)] * 4,
    )(counts, sources)


def potential_kernel(kind, step, per_device, pieces, walked, me, jobs, base, slab, *refs):
    fields, refs = refs[:pieces], refs[pieces:]
    cholesky, refs = refs[0], refs[1:]
    walkers, refs = (refs[0], refs[1:]) if walked else (None, refs)
    scratch = refs[-4 - walked :]
    blocks, left, held, semaphores = scratch[:4]
    picked = scratch[4] if walked else None
    outs = refs[: -4 - walked]
    steps = (0, 1) if kind == "mixed" else (step,)
    vectors = blocks.shape[1]
    halves = semaphores.shape[0] - 1
    half_rows = blocks.shape[2] // halves
    orbitals = blocks.shape[3]
    devices = held.shape[0]
    block = pl.program_id(0)

    members = {0: range(devices), 1: range(1, devices, 2)}
    if kind != "mixed":
        members = {step: range(devices if kind == "all" else devices // 2)}

    def slot_of(number):
        if kind == "all":
            return jobs[step, base[0] + number // 2 + number % 2 * (devices // 2)]
        if kind == "mixed":
            return jobs[1, number]
        return jobs[2, (me[0] // 2) ^ number]

    @pl.when(block == 0)
    def _():
        for half in range(halves):
            rows = pl.ds(half * half_rows, half_rows)
            for which, step in enumerate(steps):

                def one(vector, carry, rows=rows, half=half, which=which, step=step):
                    pltpu.make_async_copy(
                        cholesky.at[slab[step, vector], rows, :],
                        blocks.at[which, vector, rows, :],
                        semaphores.at[half],
                    ).start()
                    return carry

                lax.fori_loop(0, vectors, one, 0, unroll=8)
        if walked:
            for number in range(devices):
                pltpu.make_async_copy(
                    walkers.at[slot_of(number)], picked.at[number], semaphores.at[halves]
                ).start()
        part = devices // pieces
        for piece in range(pieces):
            held[piece * part : (piece + 1) * part, :] = fields[piece][...].astype(jnp.float32)
        widen = (
            lax.broadcasted_iota(jnp.int32, (vectors, vectors * ROWS), 0)
            == lax.broadcasted_iota(jnp.int32, (vectors, vectors * ROWS), 1) // ROWS
        )
        widen = widen.astype(jnp.float32).astype(jnp.bfloat16)
        start = 0
        for now in steps:
            shape = (len(members[now]) * ROWS, devices)
            row = lax.broadcasted_iota(jnp.int32, shape, 0) // ROWS
            column = lax.broadcasted_iota(jnp.int32, shape, 1)
            wanted = jnp.zeros(shape, jnp.int32)
            for place, number in enumerate(members[now]):
                slot = slot_of(number)
                there = ((slot // per_device) ^ me[0]) * per_device + slot % per_device
                if kind == "mixed":
                    there = jnp.where(jobs[0, number] == now, there, -1)
                wanted = jnp.where(row == place, there, wanted)
            repeated = jnp.zeros((shape[0], vectors), jnp.float32)
            for within in range(per_device):
                rows_of = (wanted == column * per_device + within).astype(jnp.float32)
                first = (now * per_device + within) * vectors
                repeated = repeated + jnp.dot(
                    rows_of.astype(jnp.bfloat16),
                    held[:, first : first + vectors].astype(jnp.bfloat16),
                    preferred_element_type=jnp.float32,
                )
            wide = jnp.dot(
                repeated.astype(jnp.bfloat16), widen, preferred_element_type=jnp.float32
            )
            same = (
                lax.broadcasted_iota(jnp.int32, wide.shape, 0) % ROWS
                == lax.broadcasted_iota(jnp.int32, wide.shape, 1) % ROWS
            )
            left[start : start + shape[0], :] = jnp.where(same, wide, 0.0).astype(jnp.bfloat16)
            start += shape[0]
        if walked:
            pltpu.make_async_copy(picked, picked, semaphores.at[halves]).wait()

    for half in range(halves):

        @pl.when(block == half * (half_rows // ROWS))
        def _():
            view = blocks.at[:, :, pl.ds(half * half_rows, half_rows), :]
            pltpu.make_async_copy(view, view, semaphores.at[half]).wait()

    rows = pl.ds(block * ROWS, ROWS)

    def product(which, first, count):
        right = blocks[which, :, rows, :].reshape(vectors * ROWS, orbitals)
        return jnp.dot(
            left[first : first + count * ROWS, :], right, preferred_element_type=jnp.float32
        )

    count = len(members[steps[0]])
    made = product(0, 0, count)
    if kind == "mixed":
        second = product(1, count * ROWS, len(members[1]))
    for number in range(count):
        value = made[number * ROWS : (number + 1) * ROWS]
        if kind == "mixed" and number % 2:
            value = value + second[number // 2 * ROWS : (number // 2 + 1) * ROWS]
        out = outs[number] if kind == "chips" else outs[0].at[number]
        out[:, :orbitals] = value.astype(jnp.bfloat16)
        if walked:
            out[:, orbitals:] = picked[number, rows, :]


def potential_rows(
    cholesky, slab, fields, walkers, jobs, me, base, kind, step, per_device, devices
):
    local_rows, orbitals = cholesky.shape[1:]
    vectors = slab.shape[1]
    count = 2 if kind == "mixed" else 1
    targets = devices // 2 if kind == "chips" else devices
    made = targets + (devices // 2 if kind == "mixed" else 0)
    walked = walkers is not None
    width = orbitals + (walkers.shape[2] if walked else 0)
    halves = 2 if local_rows % (2 * ROWS) == 0 else 1
    scratch = [
        pltpu.VMEM((count, vectors, local_rows, orbitals), jnp.bfloat16),
        pltpu.VMEM((made * ROWS, vectors * ROWS), jnp.bfloat16),
        pltpu.VMEM((devices, fields[0].shape[1]), jnp.float32),
        pltpu.SemaphoreType.DMA((halves + 1,)),
    ]
    if walked:
        scratch.append(pltpu.VMEM((targets,) + walkers.shape[1:], jnp.bfloat16))
    if kind == "chips":
        shapes = [jax.ShapeDtypeStruct((local_rows, width), jnp.bfloat16)] * targets
        specs = [pl.BlockSpec((ROWS, width), lambda block: (block, 0))] * targets
    else:
        shapes = jax.ShapeDtypeStruct((targets, local_rows, width), jnp.bfloat16)
        specs = pl.BlockSpec((targets, ROWS, width), lambda block: (0, block, 0))
    return pl.pallas_call(
        functools.partial(
            potential_kernel, kind, step, per_device, len(fields), walked
        ),
        out_shape=shapes,
        grid=(local_rows // ROWS,),
        in_specs=[SMEM] * 4 + [VMEM] * len(fields) + [ANY] * (1 + walked),
        out_specs=specs,
        scratch_shapes=scratch,
        cost_estimate=pl.CostEstimate(
            flops=2 * made * ROWS * vectors * local_rows * orbitals,
            bytes_accessed=2 * (count * vectors + targets) * local_rows * orbitals,
            transcendentals=0,
        ),
        compiler_params=params(),
    )(me, jobs, base, slab, *fields, cholesky, *((walkers,) if walked else ()))


def taylor_kernel(mode, chips, me, jobs, joint, *refs):
    parts, refs = (refs[:chips], refs[chips:]) if mode == "small" else ((), refs)
    across, refs = (refs[: chips], refs[chips:]) if mode == "small" else ((), refs)
    count = {"first": 0, "large": 1, "small": 3}[mode]
    starts, refs = refs[:count], refs[count:]
    out, matrix, begun, summed, term, semaphores, ready = refs
    devices, local = joint.shape[:2]
    rows, columns = summed.shape
    tiles = devices // 4
    tile = rows // tiles

    def view(number):
        return matrix.at[pl.ds(pl.multiple_of(number * tile, tile), tile), :]

    def copy_joint(number):
        for device in range(4):
            pltpu.make_async_copy(
                joint.at[4 * number + device, :, pl.ds(0, rows)],
                matrix.at[pl.ds(pl.multiple_of((4 * number + device) * local, local), local), :],
                semaphores.at[number],
            ).start()

    def copy_begun(source):
        pltpu.make_async_copy(source, begun, ready).start()

    if mode == "first":
        for device in range(devices):
            pltpu.make_async_copy(
                joint.at[device, :, pl.ds(rows, columns)],
                begun.at[pl.ds(device * local, local), :],
                ready,
            ).start()
    if mode == "large":
        copy_begun(starts[0])
    if mode == "small":
        own = me[0] % 2 == 0

        @pl.when(own)
        def _():
            copy_begun(starts[0])
            for chip in range(chips):
                for core in range(2):
                    device = me[0] ^ (2 * chip + core)
                    pltpu.make_async_copy(
                        across[chip] if core else parts[chip],
                        matrix.at[pl.ds(pl.multiple_of(device * local, local), local), :],
                        semaphores.at[device // 4],
                    ).start()

        @pl.when(jnp.logical_not(own))
        def _():
            twin = jobs[3, me[0] // 2] == 1
            pl.when(twin)(lambda: copy_begun(starts[1]))
            pl.when(jnp.logical_not(twin))(lambda: copy_begun(starts[2]))
            for number in range(tiles):
                copy_joint(number)
    else:
        for number in range(tiles):
            copy_joint(number)
    pltpu.make_async_copy(begun, begun, ready).wait()
    for degree in range(1, ORDER + 1):
        for number in range(tiles):
            span = slice(number * tile, (number + 1) * tile)
            if degree == 1:
                pltpu.make_async_copy(view(number), view(number), semaphores.at[number]).wait()
                source = begun[...]
                before = begun[span, :].astype(jnp.float32)
            else:
                source = term[degree % 2]
                before = summed[span, :]
            product = jnp.dot(
                matrix[span, :], source, preferred_element_type=jnp.float32
            ) * (1.0 / degree)
            if degree < ORDER:
                summed[span, :] = before + product
                term[(degree + 1) % 2, span, :] = product.astype(jnp.bfloat16)
            else:
                out[span, :] = (before + product).astype(jnp.bfloat16)


def taylor(mode, me, jobs, joint, parts, across, starts, columns):
    devices, local = joint.shape[:2]
    rows = devices * local
    chips = devices // 2
    return pl.pallas_call(
        functools.partial(taylor_kernel, mode, chips),
        out_shape=jax.ShapeDtypeStruct((rows, columns), jnp.bfloat16),
        in_specs=[SMEM] * 2 + [ANY] * (1 + len(parts) + len(across) + len(starts)),
        out_specs=VMEM,
        scratch_shapes=[
            pltpu.VMEM((rows, rows), jnp.bfloat16),
            pltpu.VMEM((rows, columns), jnp.bfloat16),
            pltpu.VMEM((rows, columns), jnp.float32),
            pltpu.VMEM((2, rows, columns), jnp.bfloat16),
            pltpu.SemaphoreType.DMA((devices // 4,)),
            pltpu.SemaphoreType.DMA,
        ],
        cost_estimate=pl.CostEstimate(
            flops=2 * ORDER * rows * rows * columns,
            bytes_accessed=2 * rows * (rows + 3 * columns),
            transcendentals=0,
        ),
        compiler_params=params(),
    )(me, jobs, joint, *parts, *across, *starts)


def select_kernel(small, kept, place, base, returned, *refs):
    out = refs[-1]
    devices = returned.shape[0]

    def one(slot, carry):
        chain = place[slot] - base[0]
        hit = jnp.logical_and(chain >= 0, chain < devices)
        owner = jnp.clip(chain, 0, devices - 1)
        if not small:
            owner = owner % (devices // 2) * 2 + owner // (devices // 2)

        @pl.when(hit)
        def _():
            out[slot] = returned[owner]

        @pl.when(jnp.logical_not(hit))
        def _():
            out[slot] = refs[0][slot] if kept else jnp.zeros(out.shape[1:], out.dtype)

        return carry

    lax.fori_loop(0, out.shape[0], one, 0)


def select(place, base, returned, before, small):
    kept = before is not None
    shape = place.shape + returned.shape[1:]
    return pl.pallas_call(
        functools.partial(select_kernel, small, kept),
        out_shape=jax.ShapeDtypeStruct(shape, returned.dtype),
        in_specs=[SMEM] * 2 + [VMEM] * (1 + kept),
        out_specs=VMEM,
        compiler_params=params(),
    )(place, base, returned, *((before,) if kept else ()))


def swap(array, distance, devices, senders=lambda device: True):
    pairs = [(d, d ^ distance) for d in range(devices) if senders(d)]
    return lax.ppermute(array, "row", pairs)


def share_fields(fields, devices):
    rows, distance = fields.reshape(1, -1), 1
    while distance * 4 < devices:
        rows = jnp.concatenate([rows, swap(rows, distance, devices)])
        distance *= 2
    return [rows] + [swap(rows, far, devices) for far in range(distance, devices, distance)]


def by_chips(walkers, cholesky, slab_index, fields, counts, sources):
    local_rows, columns = walkers.shape[1:]
    per_device = fields.shape[1]
    devices = lax.axis_size("row")
    chips = devices // 2
    me = lax.axis_index("row").reshape(1).astype(jnp.int32)
    lists, place, jobs, owned, total = plan(counts, sources, per_device)
    pieces = share_fields(fields, devices)

    def one_pass(small, base, before):
        def rows_of(kind, step, moved):
            return potential_rows(
                cholesky, slab_index, pieces, moved, lists if kind == "all" else jobs, me,
                base, kind, step, per_device, devices,
            )

        rows = rows_of("mixed" if small else "all", 0, walkers)
        joint = exchange(rows)
        if small:
            late = rows_of("chips", 1, None)
            parts = [late[0]] + [
                swap(late[m], 2 * m, devices, lambda d: d % 2 == 0)
                for m in range(1, chips)
            ]
            across = [swap(late[m], 2 * m + 1, devices, lambda d: d % 2 == 1) for m in range(chips)]
            current = taylor("first", me, jobs, joint, [], [], [], columns)
            twin = swap(current, 1, devices, lambda d: d % 2 == 0)
            moved = swap(current, 2, devices, lambda d: d % 4 == 1)
            starts = [current, twin, moved]
            advanced = taylor("small", me, jobs, joint, parts, across, starts, columns)
        else:
            rows = rows_of("all", 1, None)
            late = exchange(rows)
            current = taylor("first", me, jobs, joint, [], [], [], columns)
            advanced = taylor("large", me, jobs, late, [], [], [current], columns)
        returned = exchange(advanced.reshape(devices, local_rows, columns))
        return select(owned if small else place, base, returned, before, small)

    def small():
        return one_pass(True, jnp.zeros((1,), jnp.int32), None)

    def large():
        def another(turn, before):
            return one_pass(False, jnp.full((1,), turn * devices, jnp.int32), before)

        turns = (total[0] + devices - 1) // devices
        return lax.fori_loop(0, turns, another, jnp.zeros_like(walkers))

    return lax.cond(total[1] == 1, small, large)


def exchange(array):
    return lax.all_to_all(array, "row", split_axis=0, concat_axis=0, tiled=True)


def taylor_step(potential, initial):
    summed = initial.astype(jnp.float32)
    term_now = initial
    for degree in range(1, ORDER + 1):
        product = jnp.dot(potential, term_now, preferred_element_type=jnp.float32) / degree
        summed = summed + product
        term_now = product.astype(jnp.bfloat16)
    return summed.astype(jnp.bfloat16)


def by_all_to_alls(walkers, cholesky, slab_index, fields, counts, sources):
    local_rows, columns = walkers.shape[1:]
    orbitals = cholesky.shape[2]
    per_device = fields.shape[1]
    devices = lax.axis_size("row")
    (first, second), place, _, _, total = plan(counts, sources, per_device)
    all_fields = lax.all_gather(fields, "row", axis=1, tiled=True)

    def rows_of(chosen, step, base):
        members = lax.dynamic_slice_in_dim(chosen, base, devices)
        vectors = jnp.take(cholesky, slab_index[step], axis=0, mode="clip")
        rows = jnp.dot(
            jnp.take(all_fields[step], members, axis=0, mode="clip"),
            vectors.reshape(vectors.shape[0], -1),
            preferred_element_type=jnp.float32,
        )
        return rows.astype(jnp.bfloat16).reshape(devices, local_rows, orbitals)

    def another(turn, before):
        base = turn * devices
        members = lax.dynamic_slice_in_dim(first, base, devices)
        current = exchange(jnp.take(walkers, members, axis=0, mode="clip"))
        current = current.reshape(orbitals, columns)
        for step, chosen in enumerate((first, second)):
            matrix = exchange(rows_of(chosen, step, base))
            current = taylor_step(matrix.reshape(orbitals, orbitals), current)
        returned = exchange(current.reshape(devices, local_rows, columns))
        own = place - base
        hit = jnp.logical_and(own >= 0, own < devices)
        rows = jnp.take(returned, own, axis=0, mode="clip")
        return jnp.where(hit[:, None, None], rows, before)

    turns = (total[0] + devices - 1) // devices
    return lax.fori_loop(0, turns, another, jnp.zeros_like(walkers))


def on_device(walkers, cholesky, slab_index, fields, counts, sources):
    devices = lax.axis_size("row")
    power = devices & (devices - 1) == 0
    if power and 8 <= devices <= 32 and cholesky.shape[1] % ROWS == 0 and walkers.shape[2] % 128 == 0:
        route = by_chips
    else:
        route = by_all_to_alls
    return route(walkers, cholesky, slab_index, fields, counts, sources)


def solution(mesh):
    in_specs = (
        P("groups", "row", None),
        P("groups", "row", None),
        P("groups", None),
        P(None, ("groups", "row"), None),
        P("groups"),
        P("groups", None),
    )
    out_specs = P("groups", "row", None)
    return jax.shard_map(
        on_device, mesh=mesh, in_specs=in_specs, out_specs=out_specs, check_vma=False
    )
```

```python
import functools

import jax
import jax.numpy as jnp
from jax import lax
from jax.experimental import pallas as pl
from jax.experimental.pallas import tpu as pltpu
from jax.sharding import PartitionSpec as P


ORDER = 4
ROWS = 16
SMEM = pl.BlockSpec(memory_space=pltpu.SMEM)
VMEM = pl.BlockSpec(memory_space=pltpu.VMEM)
ANY = pl.BlockSpec(memory_space=pl.ANY)


def params(mebibytes=40):
    return pltpu.CompilerParams(vmem_limit_bytes=mebibytes << 20)


def plan_kernel(
    per_device, counts, sources, lists, place, jobs, owned, total, order, lead, twin, owner
):
    slots, devices = place.shape[0], counts.shape[0]
    chips = devices // 2

    def clear(slot, carry):
        order[slot] = -1
        lead[slot] = -1
        lists[0, slot] = 0
        lists[1, slot] = 0
        return carry

    lax.fori_loop(0, slots, clear, 0, unroll=8)

    def alive(slot):
        return slot % per_device < counts[slot // per_device]

    def mark(slot, carry):
        @pl.when(alive(slot))
        def _():
            order[sources[1, slot]] = 0

        return carry

    lax.fori_loop(0, slots, mark, 0, unroll=8)

    def number(slot, found):
        count, twins = found
        kept = order[slot] >= 0
        start = sources[0, slot]
        other = lead[start]
        paired = jnp.logical_and(kept, other >= 0)

        @pl.when(kept)
        def _():
            order[slot] = count
            lists[0, count] = start
            lists[1, count] = slot

        @pl.when(paired)
        def _():
            twin[other] = count
            twin[count] = -2
            lead[start] = -1

        @pl.when(jnp.logical_and(kept, other < 0))
        def _():
            twin[count] = -1
            lead[start] = count

        return count + kept.astype(jnp.int32), twins + paired.astype(jnp.int32)

    count, twins = lax.fori_loop(
        0, slots, number, (jnp.int32(0), jnp.int32(0)), unroll=4
    )
    total[0] = count
    leads, pair = count - twins, (twins + 1) // 2
    fits = leads - chips <= jnp.maximum(chips // 2 - pair, 0)
    total[1] = fits.astype(jnp.int32)

    def empty(device, carry):
        for row in range(4):
            jobs[row, device] = 0
        return carry

    lax.fori_loop(0, devices, empty, 0, unroll=8)

    @pl.when(fits)
    def _():
        def assign(chain, taken):
            with_twin, without, more = taken
            other = twin[chain]
            leading = other > -2
            doubled = other >= 0
            single = other == -1
            chip = jnp.where(doubled, with_twin, without)
            inside = jnp.logical_and(leading, chip < chips)
            outside = jnp.logical_and(single, chip >= chips)

            @pl.when(inside)
            def _():
                jobs[1, 2 * chip] = lists[0, chain]
                jobs[2, chip] = lists[1, chain]
                owner[chain] = 2 * chip

            @pl.when(doubled)
            def _():
                jobs[0, 2 * chip + 1] = 1
                jobs[1, 2 * chip + 1] = lists[1, other]
                jobs[3, chip] = 1
                owner[other] = 2 * chip + 1

            @pl.when(outside)
            def _():
                jobs[1, 4 * more + 1] = lists[0, chain]
                jobs[0, 4 * more + 3] = 1
                jobs[1, 4 * more + 3] = lists[1, chain]
                owner[chain] = 4 * more + 3

            return (
                with_twin + doubled.astype(jnp.int32),
                without + jnp.logical_and(single, inside).astype(jnp.int32),
                more + outside.astype(jnp.int32),
            )

        lax.fori_loop(0, count, assign, (jnp.int32(0), twins, pair))

    def look(slot, carry):
        chain = jnp.where(alive(slot), order[sources[1, slot]], -1)
        place[slot] = chain
        owned[slot] = jnp.where(
            jnp.logical_and(chain >= 0, fits), owner[jnp.maximum(chain, 0)], -1
        )
        return carry

    lax.fori_loop(0, slots, look, 0, unroll=8)


def plan(counts, sources, per_device):
    slots, devices = sources.shape[1], counts.shape[0]
    vector = jax.ShapeDtypeStruct((slots,), jnp.int32)
    return pl.pallas_call(
        functools.partial(plan_kernel, per_device),
        out_shape=(
            jax.ShapeDtypeStruct((2, slots), jnp.int32),
            vector,
            jax.ShapeDtypeStruct((4, devices), jnp.int32),
            vector,
            jax.ShapeDtypeStruct((2,), jnp.int32),
        ),
        in_specs=[SMEM, SMEM],
        out_specs=(SMEM,) * 5,
        scratch_shapes=[pltpu.SMEM((slots,), jnp.int32)] * 4,
    )(counts, sources)


def potential_kernel(kind, step, per_device, pieces, walked, me, jobs, base, slab, *refs):
    fields, refs = refs[:pieces], refs[pieces:]
    cholesky, refs = refs[0], refs[1:]
    walkers, refs = (refs[0], refs[1:]) if walked else (None, refs)
    scratch = refs[-4 - walked :]
    blocks, left, held, semaphores = scratch[:4]
    picked = scratch[4] if walked else None
    outs = refs[: -4 - walked]
    steps = (step,) if kind == "chips" else (0, 1)
    vectors = blocks.shape[1]
    quarters = semaphores.shape[0] - 1
    part_rows = blocks.shape[2] // quarters
    orbitals = blocks.shape[3]
    devices = held.shape[0]
    block = pl.program_id(0)

    members = {0: range(devices), 1: range(1, devices, 2)}
    if kind == "all":
        members = {0: range(devices), 1: range(devices)}
    if kind == "chips":
        members = {step: range(devices // 2)}

    def slot_of(number, now=0):
        if kind == "all":
            return jobs[now, base[0] + number // 2 + number % 2 * (devices // 2)]
        if kind == "mixed":
            return jobs[1, number]
        return jobs[2, (me[0] // 2) ^ number]

    @pl.when(block == 0)
    def _():
        for quarter in range(quarters):
            rows = pl.ds(quarter * part_rows, part_rows)
            for which, step in enumerate(steps):

                def one(vector, carry, rows=rows, quarter=quarter, which=which, step=step):
                    pltpu.make_async_copy(
                        cholesky.at[slab[step, vector], rows, :],
                        blocks.at[which, vector, rows, :],
                        semaphores.at[quarter],
                    ).start()
                    return carry

                lax.fori_loop(0, vectors, one, 0, unroll=8)
        if walked:
            for number in range(devices):
                pltpu.make_async_copy(
                    walkers.at[slot_of(number)], picked.at[number], semaphores.at[quarters]
                ).start()
        part = devices // pieces
        for piece in range(pieces):
            held[piece * part : (piece + 1) * part, :] = fields[piece][...].astype(jnp.float32)
        widen = (
            lax.broadcasted_iota(jnp.int32, (vectors, vectors * ROWS), 0)
            == lax.broadcasted_iota(jnp.int32, (vectors, vectors * ROWS), 1) // ROWS
        )
        widen = widen.astype(jnp.float32).astype(jnp.bfloat16)
        start = 0
        for now in steps:
            shape = (len(members[now]) * ROWS, devices)
            row = lax.broadcasted_iota(jnp.int32, shape, 0) // ROWS
            column = lax.broadcasted_iota(jnp.int32, shape, 1)
            wanted = jnp.zeros(shape, jnp.int32)
            for place, number in enumerate(members[now]):
                slot = slot_of(number, now)
                there = ((slot // per_device) ^ me[0]) * per_device + slot % per_device
                if kind == "mixed":
                    there = jnp.where(jobs[0, number] == now, there, -1)
                wanted = jnp.where(row == place, there, wanted)
            repeated = jnp.zeros((shape[0], vectors), jnp.float32)
            for within in range(per_device):
                rows_of = (wanted == column * per_device + within).astype(jnp.float32)
                first = (now * per_device + within) * vectors
                repeated = repeated + jnp.dot(
                    rows_of.astype(jnp.bfloat16),
                    held[:, first : first + vectors].astype(jnp.bfloat16),
                    preferred_element_type=jnp.float32,
                )
            wide = jnp.dot(
                repeated.astype(jnp.bfloat16), widen, preferred_element_type=jnp.float32
            )
            same = (
                lax.broadcasted_iota(jnp.int32, wide.shape, 0) % ROWS
                == lax.broadcasted_iota(jnp.int32, wide.shape, 1) % ROWS
            )
            left[start : start + shape[0], :] = jnp.where(same, wide, 0.0).astype(jnp.bfloat16)
            start += shape[0]
        if walked:
            pltpu.make_async_copy(picked, picked, semaphores.at[quarters]).wait()

    for quarter in range(quarters):

        @pl.when(block == quarter * (part_rows // ROWS))
        def _():
            view = blocks.at[:, :, pl.ds(quarter * part_rows, part_rows), :]
            pltpu.make_async_copy(view, view, semaphores.at[quarter]).wait()

    rows = pl.ds(block * ROWS, ROWS)

    def product(which, first, count):
        right = blocks[which, :, rows, :].reshape(vectors * ROWS, orbitals)
        return jnp.dot(
            left[first : first + count * ROWS, :], right, preferred_element_type=jnp.float32
        )

    count = len(members[steps[0]])
    made = product(0, 0, count)
    if kind != "chips":
        second = product(1, count * ROWS, len(members[1]))
    for number in range(count):
        value = made[number * ROWS : (number + 1) * ROWS]
        if kind == "mixed" and number % 2:
            value = value + second[number // 2 * ROWS : (number // 2 + 1) * ROWS]
        out = outs[number] if kind == "chips" else outs[0].at[number]
        width = out.shape[1]
        out[:, :orbitals] = value.astype(jnp.bfloat16)
        if kind == "all":
            value = second[number * ROWS : (number + 1) * ROWS]
            out[:, orbitals : 2 * orbitals] = value.astype(jnp.bfloat16)
        if walked:
            out[:, width - picked.shape[2] :] = picked[number, rows, :]


def potential_rows(
    cholesky, slab, fields, walkers, jobs, me, base, kind, step, per_device, devices
):
    local_rows, orbitals = cholesky.shape[1:]
    vectors = slab.shape[1]
    count = 1 if kind == "chips" else 2
    targets = devices // 2 if kind == "chips" else devices
    made = targets + {"chips": 0, "mixed": devices // 2, "all": devices}[kind]
    walked = walkers is not None
    width = orbitals * (1 + (kind == "all")) + (walkers.shape[2] if walked else 0)
    quarters = next(n for n in (4, 2, 1) if local_rows % (n * ROWS) == 0)
    scratch = [
        pltpu.VMEM((count, vectors, local_rows, orbitals), jnp.bfloat16),
        pltpu.VMEM((made * ROWS, vectors * ROWS), jnp.bfloat16),
        pltpu.VMEM((devices, fields[0].shape[1]), jnp.float32),
        pltpu.SemaphoreType.DMA((quarters + 1,)),
    ]
    if walked:
        scratch.append(pltpu.VMEM((targets,) + walkers.shape[1:], jnp.bfloat16))
    if kind == "chips":
        shapes = [jax.ShapeDtypeStruct((local_rows, width), jnp.bfloat16)] * targets
        specs = [pl.BlockSpec((ROWS, width), lambda block: (block, 0))] * targets
    else:
        shapes = jax.ShapeDtypeStruct((targets, local_rows, width), jnp.bfloat16)
        specs = pl.BlockSpec((targets, ROWS, width), lambda block: (0, block, 0))
    return pl.pallas_call(
        functools.partial(
            potential_kernel, kind, step, per_device, len(fields), walked
        ),
        out_shape=shapes,
        grid=(local_rows // ROWS,),
        in_specs=[SMEM] * 4 + [VMEM] * len(fields) + [ANY] * (1 + walked),
        out_specs=specs,
        scratch_shapes=scratch,
        cost_estimate=pl.CostEstimate(
            flops=2 * made * ROWS * vectors * local_rows * orbitals,
            bytes_accessed=2 * (count * vectors + targets) * local_rows * orbitals,
            transcendentals=0,
        ),
        compiler_params=params(),
    )(me, jobs, base, slab, *fields, cholesky, *((walkers,) if walked else ()))


def taylor_kernel(mode, chips, me, jobs, joint, *refs):
    parts, refs = (refs[:chips], refs[chips:]) if mode == "small" else ((), refs)
    across, refs = (refs[: chips], refs[chips:]) if mode == "small" else ((), refs)
    count = {"first": 0, "large": 1, "small": 3}[mode]
    starts, refs = refs[:count], refs[count:]
    out, matrix, begun, summed, term, semaphores, ready = refs
    devices, local = joint.shape[:2]
    rows, columns = summed.shape
    tiles = devices // 4
    tile = rows // tiles

    def view(number):
        return matrix.at[pl.ds(pl.multiple_of(number * tile, tile), tile), :]

    def copy_joint(number):
        for device in range(4):
            pltpu.make_async_copy(
                joint.at[4 * number + device, :, pl.ds(rows if mode == "large" else 0, rows)],
                matrix.at[pl.ds(pl.multiple_of((4 * number + device) * local, local), local), :],
                semaphores.at[number],
            ).start()

    def copy_begun(source):
        pltpu.make_async_copy(source, begun, ready).start()

    if mode == "first":
        for device in range(devices):
            pltpu.make_async_copy(
                joint.at[device, :, pl.ds(joint.shape[2] - columns, columns)],
                begun.at[pl.ds(device * local, local), :],
                ready,
            ).start()
    if mode == "large":
        copy_begun(starts[0])
    if mode == "small":
        own = me[0] % 2 == 0

        @pl.when(own)
        def _():
            copy_begun(starts[0])
            for chip in range(chips):
                for core in range(2):
                    device = me[0] ^ (2 * chip + core)
                    pltpu.make_async_copy(
                        across[chip] if core else parts[chip],
                        matrix.at[pl.ds(pl.multiple_of(device * local, local), local), :],
                        semaphores.at[device // 4],
                    ).start()

        @pl.when(jnp.logical_not(own))
        def _():
            twin = jobs[3, me[0] // 2] == 1
            pl.when(twin)(lambda: copy_begun(starts[1]))
            pl.when(jnp.logical_not(twin))(lambda: copy_begun(starts[2]))
            for number in range(tiles):
                copy_joint(number)
    else:
        for number in range(tiles):
            copy_joint(number)
    pltpu.make_async_copy(begun, begun, ready).wait()
    for degree in range(1, ORDER + 1):
        for number in range(tiles):
            span = slice(number * tile, (number + 1) * tile)
            if degree == 1:
                pltpu.make_async_copy(view(number), view(number), semaphores.at[number]).wait()
                source = begun[...]
                before = begun[span, :].astype(jnp.float32)
            else:
                source = term[degree % 2]
                before = summed[span, :]
            product = jnp.dot(
                matrix[span, :], source, preferred_element_type=jnp.float32
            ) * (1.0 / degree)
            if degree < ORDER:
                summed[span, :] = before + product
                term[(degree + 1) % 2, span, :] = product.astype(jnp.bfloat16)
            else:
                out[span, :] = (before + product).astype(jnp.bfloat16)


def taylor(mode, me, jobs, joint, parts, across, starts, columns):
    devices, local = joint.shape[:2]
    rows = devices * local
    chips = devices // 2
    return pl.pallas_call(
        functools.partial(taylor_kernel, mode, chips),
        out_shape=jax.ShapeDtypeStruct((rows, columns), jnp.bfloat16),
        in_specs=[SMEM] * 2 + [ANY] * (1 + len(parts) + len(across) + len(starts)),
        out_specs=VMEM,
        scratch_shapes=[
            pltpu.VMEM((rows, rows), jnp.bfloat16),
            pltpu.VMEM((rows, columns), jnp.bfloat16),
            pltpu.VMEM((rows, columns), jnp.float32),
            pltpu.VMEM((2, rows, columns), jnp.bfloat16),
            pltpu.SemaphoreType.DMA((devices // 4,)),
            pltpu.SemaphoreType.DMA,
        ],
        cost_estimate=pl.CostEstimate(
            flops=2 * ORDER * rows * rows * columns,
            bytes_accessed=2 * rows * (rows + 3 * columns),
            transcendentals=0,
        ),
        compiler_params=params(),
    )(me, jobs, joint, *parts, *across, *starts)


def select_kernel(small, kept, place, base, returned, *refs):
    out = refs[-1]
    devices = returned.shape[0]

    def one(slot, carry):
        chain = place[slot] - base[0]
        hit = jnp.logical_and(chain >= 0, chain < devices)
        owner = jnp.clip(chain, 0, devices - 1)
        if not small:
            owner = owner % (devices // 2) * 2 + owner // (devices // 2)

        @pl.when(hit)
        def _():
            out[slot] = returned[owner]

        @pl.when(jnp.logical_not(hit))
        def _():
            out[slot] = refs[0][slot] if kept else jnp.zeros(out.shape[1:], out.dtype)

        return carry

    lax.fori_loop(0, out.shape[0], one, 0)


def select(place, base, returned, before, small):
    kept = before is not None
    shape = place.shape + returned.shape[1:]
    return pl.pallas_call(
        functools.partial(select_kernel, small, kept),
        out_shape=jax.ShapeDtypeStruct(shape, returned.dtype),
        in_specs=[SMEM] * 2 + [VMEM] * (1 + kept),
        out_specs=VMEM,
        compiler_params=params(),
    )(place, base, returned, *((before,) if kept else ()))


def swap(array, distance, devices, senders=lambda device: True):
    pairs = [(d, d ^ distance) for d in range(devices) if senders(d)]
    return lax.ppermute(array, "row", pairs)


def share_fields(fields, devices):
    rows, distance = fields.reshape(1, -1), 1
    while distance * 4 < devices:
        rows = jnp.concatenate([rows, swap(rows, distance, devices)])
        distance *= 2
    return [rows] + [swap(rows, far, devices) for far in range(distance, devices, distance)]


def by_chips(walkers, cholesky, slab_index, fields, counts, sources):
    local_rows, columns = walkers.shape[1:]
    per_device = fields.shape[1]
    devices = lax.axis_size("row")
    chips = devices // 2
    me = lax.axis_index("row").reshape(1).astype(jnp.int32)
    lists, place, jobs, owned, total = plan(counts, sources, per_device)
    pieces = share_fields(fields, devices)

    def one_pass(small, base, before):
        def rows_of(kind, step, moved):
            return potential_rows(
                cholesky, slab_index, pieces, moved, lists if kind == "all" else jobs, me,
                base, kind, step, per_device, devices,
            )

        rows = rows_of("mixed" if small else "all", 0, walkers)
        joint = exchange(rows)
        if small:
            late = rows_of("chips", 1, None)
            parts = [late[0]] + [
                swap(late[m], 2 * m, devices, lambda d: d % 2 == 0)
                for m in range(1, chips)
            ]
            across = [swap(late[m], 2 * m + 1, devices, lambda d: d % 2 == 1) for m in range(chips)]
            current = taylor("first", me, jobs, joint, [], [], [], columns)
            twin = swap(current, 1, devices, lambda d: d % 2 == 0)
            moved = swap(current, 2, devices, lambda d: d % 4 == 1)
            starts = [current, twin, moved]
            advanced = taylor("small", me, jobs, joint, parts, across, starts, columns)
        else:
            current = taylor("first", me, jobs, joint, [], [], [], columns)
            advanced = taylor("large", me, jobs, joint, [], [], [current], columns)
        returned = exchange(advanced.reshape(devices, local_rows, columns))
        return select(owned if small else place, base, returned, before, small)

    def small():
        return one_pass(True, jnp.zeros((1,), jnp.int32), None)

    def large():
        return one_pass(False, jnp.zeros((1,), jnp.int32), None)

    def huge():
        def another(turn, before):
            return one_pass(False, jnp.full((1,), turn * devices, jnp.int32), before)

        turns = (total[0] + devices - 1) // devices
        return lax.fori_loop(0, turns, another, jnp.zeros_like(walkers))

    fitting = jnp.where(total[0] <= devices, 1, 2)
    return lax.switch(jnp.where(total[1] == 1, 0, fitting), [small, large, huge])


def exchange(array):
    return lax.all_to_all(array, "row", split_axis=0, concat_axis=0, tiled=True)


def taylor_step(potential, initial):
    summed = initial.astype(jnp.float32)
    term_now = initial
    for degree in range(1, ORDER + 1):
        product = jnp.dot(potential, term_now, preferred_element_type=jnp.float32) / degree
        summed = summed + product
        term_now = product.astype(jnp.bfloat16)
    return summed.astype(jnp.bfloat16)


def by_all_to_alls(walkers, cholesky, slab_index, fields, counts, sources):
    local_rows, columns = walkers.shape[1:]
    orbitals = cholesky.shape[2]
    per_device = fields.shape[1]
    devices = lax.axis_size("row")
    (first, second), place, _, _, total = plan(counts, sources, per_device)
    all_fields = lax.all_gather(fields, "row", axis=1, tiled=True)

    def rows_of(chosen, step, base):
        members = lax.dynamic_slice_in_dim(chosen, base, devices)
        vectors = jnp.take(cholesky, slab_index[step], axis=0, mode="clip")
        rows = jnp.dot(
            jnp.take(all_fields[step], members, axis=0, mode="clip"),
            vectors.reshape(vectors.shape[0], -1),
            preferred_element_type=jnp.float32,
        )
        return rows.astype(jnp.bfloat16).reshape(devices, local_rows, orbitals)

    def another(turn, before):
        base = turn * devices
        members = lax.dynamic_slice_in_dim(first, base, devices)
        current = exchange(jnp.take(walkers, members, axis=0, mode="clip"))
        current = current.reshape(orbitals, columns)
        for step, chosen in enumerate((first, second)):
            matrix = exchange(rows_of(chosen, step, base))
            current = taylor_step(matrix.reshape(orbitals, orbitals), current)
        returned = exchange(current.reshape(devices, local_rows, columns))
        own = place - base
        hit = jnp.logical_and(own >= 0, own < devices)
        rows = jnp.take(returned, own, axis=0, mode="clip")
        return jnp.where(hit[:, None, None], rows, before)

    turns = (total[0] + devices - 1) // devices
    return lax.fori_loop(0, turns, another, jnp.zeros_like(walkers))


def on_device(walkers, cholesky, slab_index, fields, counts, sources):
    devices = lax.axis_size("row")
    power = devices & (devices - 1) == 0
    if power and 8 <= devices <= 32 and cholesky.shape[1] % ROWS == 0 and walkers.shape[2] % 128 == 0:
        route = by_chips
    else:
        route = by_all_to_alls
    return route(walkers, cholesky, slab_index, fields, counts, sources)


def solution(mesh):
    in_specs = (
        P("groups", "row", None),
        P("groups", "row", None),
        P("groups", None),
        P(None, ("groups", "row"), None),
        P("groups"),
        P("groups", None),
    )
    out_specs = P("groups", "row", None)
    return jax.shard_map(
        on_device, mesh=mesh, in_specs=in_specs, out_specs=out_specs, check_vma=False
    )
```

```python
import functools
import itertools

import jax
import jax.numpy as jnp
from jax import lax
from jax.experimental import pallas as pl
from jax.experimental.pallas import tpu as pltpu
from jax.sharding import PartitionSpec as P


ORDER = 4
ROWS = 16
SMEM = pl.BlockSpec(memory_space=pltpu.SMEM)
VMEM = pl.BlockSpec(memory_space=pltpu.VMEM)
ANY = pl.BlockSpec(memory_space=pl.ANY)


def params(mebibytes=40):
    return pltpu.CompilerParams(vmem_limit_bytes=mebibytes << 20)


def plan_kernel(
    per_device, counts, sources, lists, place, jobs, owned, total, order, lead, twin, owner
):
    slots, devices = place.shape[0], counts.shape[0]
    chips = devices // 2

    def clear(slot, carry):
        order[slot] = -1
        lead[slot] = -1
        lists[0, slot] = 0
        lists[1, slot] = 0
        return carry

    lax.fori_loop(0, slots, clear, 0, unroll=8)

    def alive(slot):
        return slot % per_device < counts[slot // per_device]

    def mark(slot, carry):
        @pl.when(alive(slot))
        def _():
            order[sources[1, slot]] = 0

        return carry

    lax.fori_loop(0, slots, mark, 0, unroll=8)

    def number(slot, found):
        count, twins = found
        kept = order[slot] >= 0
        start = sources[0, slot]
        other = lead[start]
        paired = jnp.logical_and(kept, other >= 0)

        @pl.when(kept)
        def _():
            order[slot] = count
            lists[0, count] = start
            lists[1, count] = slot

        @pl.when(paired)
        def _():
            twin[other] = count
            twin[count] = -2
            lead[start] = -1

        @pl.when(jnp.logical_and(kept, other < 0))
        def _():
            twin[count] = -1
            lead[start] = count

        return count + kept.astype(jnp.int32), twins + paired.astype(jnp.int32)

    count, twins = lax.fori_loop(
        0, slots, number, (jnp.int32(0), jnp.int32(0)), unroll=4
    )
    total[0] = count
    leads, pair = count - twins, (twins + 1) // 2
    fits = leads - chips <= jnp.maximum(chips // 2 - pair, 0)
    total[1] = fits.astype(jnp.int32)

    def empty(device, carry):
        for row in range(4):
            jobs[row, device] = 0
        return carry

    lax.fori_loop(0, devices, empty, 0, unroll=8)

    @pl.when(fits)
    def _():
        def assign(chain, taken):
            with_twin, without, more = taken
            other = twin[chain]
            leading = other > -2
            doubled = other >= 0
            single = other == -1
            chip = jnp.where(doubled, with_twin, without)
            inside = jnp.logical_and(leading, chip < chips)
            outside = jnp.logical_and(single, chip >= chips)

            @pl.when(inside)
            def _():
                jobs[1, 2 * chip] = lists[0, chain]
                jobs[2, chip] = lists[1, chain]
                owner[chain] = 2 * chip

            @pl.when(doubled)
            def _():
                jobs[0, 2 * chip + 1] = 1
                jobs[1, 2 * chip + 1] = lists[1, other]
                jobs[3, chip] = 1
                owner[other] = 2 * chip + 1

            @pl.when(outside)
            def _():
                jobs[1, 4 * more + 1] = lists[0, chain]
                jobs[0, 4 * more + 3] = 1
                jobs[1, 4 * more + 3] = lists[1, chain]
                owner[chain] = 4 * more + 3

            return (
                with_twin + doubled.astype(jnp.int32),
                without + jnp.logical_and(single, inside).astype(jnp.int32),
                more + outside.astype(jnp.int32),
            )

        lax.fori_loop(0, count, assign, (jnp.int32(0), twins, pair))

    def look(slot, carry):
        chain = jnp.where(alive(slot), order[sources[1, slot]], -1)
        place[slot] = chain
        owned[slot] = jnp.where(
            jnp.logical_and(chain >= 0, fits), owner[jnp.maximum(chain, 0)], -1
        )
        return carry

    lax.fori_loop(0, slots, look, 0, unroll=8)


def plan(counts, sources, per_device):
    slots, devices = sources.shape[1], counts.shape[0]
    vector = jax.ShapeDtypeStruct((slots,), jnp.int32)
    return pl.pallas_call(
        functools.partial(plan_kernel, per_device),
        out_shape=(
            jax.ShapeDtypeStruct((2, slots), jnp.int32),
            vector,
            jax.ShapeDtypeStruct((4, devices), jnp.int32),
            vector,
            jax.ShapeDtypeStruct((2,), jnp.int32),
        ),
        in_specs=[SMEM, SMEM],
        out_specs=(SMEM,) * 5,
        scratch_shapes=[pltpu.SMEM((slots,), jnp.int32)] * 4,
    )(counts, sources)


def potential_kernel(kind, step, per_device, pieces, walked, me, jobs, base, slab, *refs):
    fields, refs = refs[:pieces], refs[pieces:]
    cholesky, refs = refs[0], refs[1:]
    walkers, refs = (refs[0], refs[1:]) if walked else (None, refs)
    scratch = refs[-4 - walked :]
    blocks, left, held, semaphores = scratch[:4]
    picked = scratch[4] if walked else None
    outs = refs[: -4 - walked]
    steps = (step,) if kind == "chips" else (0, 1)
    vectors = blocks.shape[1]
    quarters = semaphores.shape[0] - 1
    part_rows = blocks.shape[2] // quarters
    orbitals = blocks.shape[3]
    devices = held.shape[0]
    block = pl.program_id(0)

    members = {0: range(devices), 1: range(1, devices, 2)}
    if kind == "all":
        members = {0: range(devices), 1: range(devices)}
    if kind == "chips":
        members = {step: range(devices // 2)}

    def slot_of(number, now=0):
        if kind == "all":
            return jobs[now, base[0] + number // 2 + number % 2 * (devices // 2)]
        if kind == "mixed":
            return jobs[1, number]
        return jobs[2, (me[0] // 2) ^ number]

    @pl.when(block == 0)
    def _():
        for quarter in range(quarters):
            rows = pl.ds(quarter * part_rows, part_rows)
            for which, step in enumerate(steps):

                def one(vector, carry, rows=rows, quarter=quarter, which=which, step=step):
                    pltpu.make_async_copy(
                        cholesky.at[slab[step, vector], rows, :],
                        blocks.at[which, vector, rows, :],
                        semaphores.at[quarter],
                    ).start()
                    return carry

                lax.fori_loop(0, vectors, one, 0, unroll=8)
        if walked:
            for number in range(devices):
                pltpu.make_async_copy(
                    walkers.at[slot_of(number)], picked.at[number], semaphores.at[quarters]
                ).start()
        part = devices // pieces
        for piece in range(pieces):
            held[piece * part : (piece + 1) * part, :] = fields[piece][...].astype(jnp.float32)
        widen = (
            lax.broadcasted_iota(jnp.int32, (vectors, vectors * ROWS), 0)
            == lax.broadcasted_iota(jnp.int32, (vectors, vectors * ROWS), 1) // ROWS
        )
        widen = widen.astype(jnp.float32).astype(jnp.bfloat16)
        start = 0
        for now in steps:
            shape = (len(members[now]) * ROWS, devices)
            row = lax.broadcasted_iota(jnp.int32, shape, 0) // ROWS
            column = lax.broadcasted_iota(jnp.int32, shape, 1)
            wanted = jnp.zeros(shape, jnp.int32)
            for place, number in enumerate(members[now]):
                slot = slot_of(number, now)
                there = ((slot // per_device) ^ me[0]) * per_device + slot % per_device
                if kind == "mixed":
                    there = jnp.where(jobs[0, number] == now, there, -1)
                wanted = jnp.where(row == place, there, wanted)
            repeated = jnp.zeros((shape[0], vectors), jnp.float32)
            for within in range(per_device):
                rows_of = (wanted == column * per_device + within).astype(jnp.float32)
                first = (now * per_device + within) * vectors
                repeated = repeated + jnp.dot(
                    rows_of.astype(jnp.bfloat16),
                    held[:, first : first + vectors].astype(jnp.bfloat16),
                    preferred_element_type=jnp.float32,
                )
            wide = jnp.dot(
                repeated.astype(jnp.bfloat16), widen, preferred_element_type=jnp.float32
            )
            same = (
                lax.broadcasted_iota(jnp.int32, wide.shape, 0) % ROWS
                == lax.broadcasted_iota(jnp.int32, wide.shape, 1) % ROWS
            )
            left[start : start + shape[0], :] = jnp.where(same, wide, 0.0).astype(jnp.bfloat16)
            start += shape[0]
        if walked:
            pltpu.make_async_copy(picked, picked, semaphores.at[quarters]).wait()

    for quarter in range(quarters):

        @pl.when(block == quarter * (part_rows // ROWS))
        def _():
            view = blocks.at[:, :, pl.ds(quarter * part_rows, part_rows), :]
            pltpu.make_async_copy(view, view, semaphores.at[quarter]).wait()

    rows = pl.ds(block * ROWS, ROWS)

    def product(which, first, count):
        right = blocks[which, :, rows, :].reshape(vectors * ROWS, orbitals)
        return jnp.dot(
            left[first : first + count * ROWS, :], right, preferred_element_type=jnp.float32
        )

    count = len(members[steps[0]])
    made = product(0, 0, count)
    if kind != "chips":
        second = product(1, count * ROWS, len(members[1]))
    for number in range(count):
        value = made[number * ROWS : (number + 1) * ROWS]
        if kind == "mixed" and number % 2:
            value = value + second[number // 2 * ROWS : (number // 2 + 1) * ROWS]
        out = outs[number] if kind == "chips" else outs[0].at[number]
        width = out.shape[1]
        out[:, :orbitals] = value.astype(jnp.bfloat16)
        if kind == "all":
            value = second[number * ROWS : (number + 1) * ROWS]
            out[:, orbitals : 2 * orbitals] = value.astype(jnp.bfloat16)
        if walked:
            out[:, width - picked.shape[2] :] = picked[number, rows, :]


def potential_rows(
    cholesky, slab, fields, walkers, jobs, me, base, kind, step, per_device, devices
):
    local_rows, orbitals = cholesky.shape[1:]
    vectors = slab.shape[1]
    count = 1 if kind == "chips" else 2
    targets = devices // 2 if kind == "chips" else devices
    made = targets + {"chips": 0, "mixed": devices // 2, "all": devices}[kind]
    walked = walkers is not None
    width = orbitals * (1 + (kind == "all")) + (walkers.shape[2] if walked else 0)
    quarters = next(n for n in (4, 2, 1) if local_rows % (n * ROWS) == 0)
    scratch = [
        pltpu.VMEM((count, vectors, local_rows, orbitals), jnp.bfloat16),
        pltpu.VMEM((made * ROWS, vectors * ROWS), jnp.bfloat16),
        pltpu.VMEM((devices, fields[0].shape[1]), jnp.float32),
        pltpu.SemaphoreType.DMA((quarters + 1,)),
    ]
    if walked:
        scratch.append(pltpu.VMEM((targets,) + walkers.shape[1:], jnp.bfloat16))
    if kind == "chips":
        shapes = [jax.ShapeDtypeStruct((local_rows, width), jnp.bfloat16)] * targets
        specs = [pl.BlockSpec((ROWS, width), lambda block: (block, 0))] * targets
    else:
        shapes = jax.ShapeDtypeStruct((targets, local_rows, width), jnp.bfloat16)
        specs = pl.BlockSpec((targets, ROWS, width), lambda block: (0, block, 0))
    return pl.pallas_call(
        functools.partial(
            potential_kernel, kind, step, per_device, len(fields), walked
        ),
        out_shape=shapes,
        grid=(local_rows // ROWS,),
        in_specs=[SMEM] * 4 + [VMEM] * len(fields) + [ANY] * (1 + walked),
        out_specs=specs,
        scratch_shapes=scratch,
        cost_estimate=pl.CostEstimate(
            flops=2 * made * ROWS * vectors * local_rows * orbitals,
            bytes_accessed=2 * (count * vectors + targets) * local_rows * orbitals,
            transcendentals=0,
        ),
        compiler_params=params(),
    )(me, jobs, base, slab, *fields, cholesky, *((walkers,) if walked else ()))


def taylor_kernel(mode, chips, me, jobs, joint, *refs):
    parts, refs = (refs[:chips], refs[chips:]) if mode == "small" else ((), refs)
    across, refs = (refs[: chips], refs[chips:]) if mode == "small" else ((), refs)
    count = {"first": 0, "large": 0, "small": 3}[mode]
    starts, refs = refs[:count], refs[count:]
    out, matrices, begun, summed, term, semaphores, ready = refs
    matrix = matrices.at[0]
    devices, local = joint.shape[:2]
    rows, columns = summed.shape
    tiles = devices // 4
    tile = rows // tiles

    def copy_joint(number, step=0):
        for device in range(4):
            here = pl.multiple_of((4 * number + device) * local, local)
            pltpu.make_async_copy(
                joint.at[4 * number + device, :, pl.ds(step * rows, rows)],
                matrices.at[step, pl.ds(here, local), :],
                semaphores.at[step * tiles + number],
            ).start()

    def copy_begun(source):
        pltpu.make_async_copy(source, begun, ready).start()

    if mode != "small":
        for device in range(devices):
            pltpu.make_async_copy(
                joint.at[device, :, pl.ds(joint.shape[2] - columns, columns)],
                begun.at[pl.ds(device * local, local), :],
                ready,
            ).start()
    if mode == "small":
        own = me[0] % 2 == 0

        @pl.when(own)
        def _():
            copy_begun(starts[0])
            for chip in range(chips):
                for core in range(2):
                    device = me[0] ^ (2 * chip + core)
                    pltpu.make_async_copy(
                        across[chip] if core else parts[chip],
                        matrix.at[pl.ds(pl.multiple_of(device * local, local), local), :],
                        semaphores.at[device // 4],
                    ).start()

        @pl.when(jnp.logical_not(own))
        def _():
            twin = jobs[3, me[0] // 2] == 1
            pl.when(twin)(lambda: copy_begun(starts[1]))
            pl.when(jnp.logical_not(twin))(lambda: copy_begun(starts[2]))
            for number in range(tiles):
                copy_joint((me[0] // 4) ^ number)
    else:
        for step in range(matrices.shape[0]):
            for number in range(tiles):
                copy_joint(number, step)
    pltpu.make_async_copy(begun, begun, ready).wait()
    for step, degree in itertools.product(range(matrices.shape[0]), range(1, ORDER + 1)):
        matrix = matrices.at[step]
        for number in range(tiles):
            span = slice(number * tile, (number + 1) * tile)
            if degree == 1:
                place = number
                if mode == "small":
                    place = (me[0] // 4) ^ number
                    span = pl.ds(pl.multiple_of(place * tile, tile), tile)
                rows_in = matrix.at[span, :]
                arrived = semaphores.at[step * tiles + place]
                pltpu.make_async_copy(rows_in, rows_in, arrived).wait()
                source = begun[...]
                before = begun[span, :].astype(jnp.float32)
            else:
                source = term[degree % 2]
                before = summed[span, :]
            product = jnp.dot(
                matrix[span, :], source, preferred_element_type=jnp.float32
            ) * (1.0 / degree)
            if degree < ORDER:
                summed[span, :] = before + product
                term[(degree + 1) % 2, span, :] = product.astype(jnp.bfloat16)
            else:
                done = out if step + 1 == matrices.shape[0] else begun
                done[span, :] = (before + product).astype(jnp.bfloat16)


def taylor(mode, me, jobs, joint, parts, across, starts, columns):
    devices, local = joint.shape[:2]
    rows = devices * local
    chips = devices // 2
    return pl.pallas_call(
        functools.partial(taylor_kernel, mode, chips),
        out_shape=jax.ShapeDtypeStruct((rows, columns), jnp.bfloat16),
        in_specs=[SMEM] * 2 + [ANY] * (1 + len(parts) + len(across) + len(starts)),
        out_specs=VMEM,
        scratch_shapes=[
            pltpu.VMEM((1 + (mode == "large"), rows, rows), jnp.bfloat16),
            pltpu.VMEM((rows, columns), jnp.bfloat16),
            pltpu.VMEM((rows, columns), jnp.float32),
            pltpu.VMEM((2, rows, columns), jnp.bfloat16),
            pltpu.SemaphoreType.DMA(((1 + (mode == "large")) * (devices // 4),)),
            pltpu.SemaphoreType.DMA,
        ],
        cost_estimate=pl.CostEstimate(
            flops=2 * ORDER * rows * rows * columns,
            bytes_accessed=2 * rows * (rows + 3 * columns),
            transcendentals=0,
        ),
        compiler_params=params(),
    )(me, jobs, joint, *parts, *across, *starts)


def select_kernel(small, kept, place, base, returned, *refs):
    before, refs = (refs[0], refs[1:]) if kept else (None, refs)
    out, blank, semaphore = refs
    devices = returned.shape[0]
    blank[...] = jnp.zeros(blank.shape, blank.dtype)

    def one(slot, carry):
        chain = place[slot] - base[0]
        hit = jnp.logical_and(chain >= 0, chain < devices)
        owner = jnp.clip(chain, 0, devices - 1)
        if not small:
            owner = owner % (devices // 2) * 2 + owner // (devices // 2)

        @pl.when(hit)
        def _():
            pltpu.make_async_copy(returned.at[owner], out.at[slot], semaphore).start()

        @pl.when(jnp.logical_not(hit))
        def _():
            source = before.at[slot] if kept else blank
            pltpu.make_async_copy(source, out.at[slot], semaphore).start()

        return carry

    lax.fori_loop(0, out.shape[0], one, 0)
    pltpu.make_async_copy(out, out, semaphore).wait()


def select(place, base, returned, before, small):
    kept = before is not None
    shape = place.shape + returned.shape[1:]
    return pl.pallas_call(
        functools.partial(select_kernel, small, kept),
        out_shape=jax.ShapeDtypeStruct(shape, returned.dtype),
        in_specs=[SMEM] * 2 + [VMEM] * (1 + kept),
        out_specs=ANY,
        scratch_shapes=[
            pltpu.VMEM(returned.shape[1:], returned.dtype),
            pltpu.SemaphoreType.DMA,
        ],
        compiler_params=params(),
    )(place, base, returned, *((before,) if kept else ()))


def swap(array, distance, devices, senders=lambda device: True):
    pairs = [(d, d ^ distance) for d in range(devices) if senders(d)]
    return lax.ppermute(array, "row", pairs)


def share_fields(fields, devices):
    rows, distance = fields.reshape(1, -1), 1
    while distance * 4 < devices:
        rows = jnp.concatenate([rows, swap(rows, distance, devices)])
        distance *= 2
    return [rows] + [swap(rows, far, devices) for far in range(distance, devices, distance)]


def by_chips(walkers, cholesky, slab_index, fields, counts, sources):
    local_rows, columns = walkers.shape[1:]
    per_device = fields.shape[1]
    devices = lax.axis_size("row")
    chips = devices // 2
    me = lax.axis_index("row").reshape(1).astype(jnp.int32)
    lists, place, jobs, owned, total = plan(counts, sources, per_device)
    pieces = share_fields(fields, devices)

    def one_pass(small, base, before):
        def rows_of(kind, step, moved):
            return potential_rows(
                cholesky, slab_index, pieces, moved, lists if kind == "all" else jobs, me,
                base, kind, step, per_device, devices,
            )

        rows = rows_of("mixed" if small else "all", 0, walkers)
        joint = exchange(rows)
        if small:
            late = rows_of("chips", 1, None)
            parts = [late[0]] + [
                swap(late[m], 2 * m, devices, lambda d: d % 2 == 0)
                for m in range(1, chips)
            ]
            across = [swap(late[m], 2 * m + 1, devices, lambda d: d % 2 == 1) for m in range(chips)]
            current = taylor("first", me, jobs, joint, [], [], [], columns)
            twin = swap(current, 1, devices, lambda d: d % 2 == 0)
            moved = swap(current, 2, devices, lambda d: d % 4 == 1)
            starts = [current, twin, moved]
            advanced = taylor("small", me, jobs, joint, parts, across, starts, columns)
        else:
            advanced = taylor("large", me, jobs, joint, [], [], [], columns)
        returned = exchange(advanced.reshape(devices, local_rows, columns))
        return select(owned if small else place, base, returned, before, small)

    def small():
        return one_pass(True, jnp.zeros((1,), jnp.int32), None)

    def large():
        return one_pass(False, jnp.zeros((1,), jnp.int32), None)

    def huge():
        def another(turn, before):
            return one_pass(False, jnp.full((1,), turn * devices, jnp.int32), before)

        turns = (total[0] + devices - 1) // devices
        return lax.fori_loop(0, turns, another, jnp.zeros_like(walkers))

    fitting = jnp.where(total[0] <= devices, 1, 2)
    return lax.switch(jnp.where(total[1] == 1, 0, fitting), [small, large, huge])


def exchange(array):
    return lax.all_to_all(array, "row", split_axis=0, concat_axis=0, tiled=True)


def taylor_step(potential, initial):
    summed = initial.astype(jnp.float32)
    term_now = initial
    for degree in range(1, ORDER + 1):
        product = jnp.dot(potential, term_now, preferred_element_type=jnp.float32) / degree
        summed = summed + product
        term_now = product.astype(jnp.bfloat16)
    return summed.astype(jnp.bfloat16)


def by_all_to_alls(walkers, cholesky, slab_index, fields, counts, sources):
    local_rows, columns = walkers.shape[1:]
    orbitals = cholesky.shape[2]
    per_device = fields.shape[1]
    devices = lax.axis_size("row")
    (first, second), place, _, _, total = plan(counts, sources, per_device)
    all_fields = lax.all_gather(fields, "row", axis=1, tiled=True)

    def rows_of(chosen, step, base):
        members = lax.dynamic_slice_in_dim(chosen, base, devices)
        vectors = jnp.take(cholesky, slab_index[step], axis=0, mode="clip")
        rows = jnp.dot(
            jnp.take(all_fields[step], members, axis=0, mode="clip"),
            vectors.reshape(vectors.shape[0], -1),
            preferred_element_type=jnp.float32,
        )
        return rows.astype(jnp.bfloat16).reshape(devices, local_rows, orbitals)

    def another(turn, before):
        base = turn * devices
        members = lax.dynamic_slice_in_dim(first, base, devices)
        current = exchange(jnp.take(walkers, members, axis=0, mode="clip"))
        current = current.reshape(orbitals, columns)
        for step, chosen in enumerate((first, second)):
            matrix = exchange(rows_of(chosen, step, base))
            current = taylor_step(matrix.reshape(orbitals, orbitals), current)
        returned = exchange(current.reshape(devices, local_rows, columns))
        own = place - base
        hit = jnp.logical_and(own >= 0, own < devices)
        rows = jnp.take(returned, own, axis=0, mode="clip")
        return jnp.where(hit[:, None, None], rows, before)

    turns = (total[0] + devices - 1) // devices
    return lax.fori_loop(0, turns, another, jnp.zeros_like(walkers))


def on_device(walkers, cholesky, slab_index, fields, counts, sources):
    devices = lax.axis_size("row")
    power = devices & (devices - 1) == 0
    if power and 8 <= devices <= 32 and cholesky.shape[1] % ROWS == 0 and walkers.shape[2] % 128 == 0:
        route = by_chips
    else:
        route = by_all_to_alls
    return route(walkers, cholesky, slab_index, fields, counts, sources)


def solution(mesh):
    in_specs = (
        P("groups", "row", None),
        P("groups", "row", None),
        P("groups", None),
        P(None, ("groups", "row"), None),
        P("groups"),
        P("groups", None),
    )
    out_specs = P("groups", "row", None)
    return jax.shard_map(
        on_device, mesh=mesh, in_specs=in_specs, out_specs=out_specs, check_vma=False
    )
```
